128 devices in a mesh: grp: 8 (over z, core), pair: 2 (over x_lo), tp: 8 (over y, x_hi).
Axes of the slice: x: 4 (x_hi: 2, x_lo: 2; x = x_hi * 2 + x_lo), y: 4, z: 4, core: 2. Of those that a mesh axis runs over, the one named last changes fastest.
Arguments:
- rescaled_signals: bfloat16 [2, 4096, 8192], P(None, ('grp', 'pair')), parts along dimension 1, may hold values from -6 to 6
- linear_matrix: bfloat16 [8192, 10240], P('pair', 'tp'), may hold values from -0.0625 to 0.0625
- linear_offset: bfloat16 [10240], P('tp'), may hold values from -4 to 4
- retained_turned_probes: bfloat16 [5120, 128, 1024], P(('grp', 'pair', 'tp')), parts along dimension 0, may hold values from -250 to 250
- retained_payload: bfloat16 [5120, 128, 1024], P(('grp', 'pair', 'tp')), parts along dimension 0, may hold values from -6 to 6
- filled_extents: int32 [5120], P(('grp', 'pair', 'tp')), parts along dimension 0, may hold values from 1 to 128
- prior_owner_lines: int32 [4096], P('grp'), parts along dimension 0, may hold values from 0 to 639, as said below
Outputs:
- blended_result: bfloat16 [2, 4096, 8192], P(None, ('grp', 'pair'), 'tp'), parts along dimension 1
The draws below stay inside these ranges and needn't reach their ends.
There are 8 independent parts, one for each index of `grp`. The reference program is written for one: setup_inputs(seed, part) draws one part's arguments, and reference() takes and returns one part's arrays. A program takes and returns all parts, laid end to end along the dimension named above; an argument that names none is the same for every part. Nothing has to cross between parts.
Inputs may be any that keep to these rules, and one draw needn't show every extreme that they name: `prior_owner_lines`: 512 distinct old rows.
All inputs are finite; a program needn't handle non-finite values.
Results may differ from the reference program's by a relative error of at most 0.0105.
The reference program's roundings to bfloat16 on the way count: a program that leaves them out, or rounds other values in their place, can miss the bound.
Values may be sent and summed in bfloat16 or wider, within the bound.
No kernel may reach another device: no remote copies, remote signals or barrier semaphores. Data moves between devices by JAX's collectives and lax.ppermute only.
A program may use at most 192 MiB of HBM per device.

```python
import jax
import jax.numpy as jnp

HIDDEN_BREADTHS = 8192
ASKING_STREAMS = 64
RECALL_STREAMS = 8
FOCUS_BREADTHS = 128
ASKERS_SHARING = 8
OLD_DEV = 40
PLACES_CEILING = 128
EMIT_ITERATIONS = 2
SURVIVING_LOT = 512
PRIOR_ROWS = 640


def draw_prior_owner_lines(key, part):
    tier_key, order_key, shuffle_key = jax.random.split(key, 3)
    owners = PRIOR_ROWS // OLD_DEV
    tier_draw = jax.random.randint(tier_key, (owners,), 0, 3)
    ranking = jax.random.permutation(order_key, PRIOR_ROWS).astype(jnp.int32)
    row_index = jnp.arange(PRIOR_ROWS, dtype=jnp.int32)
    boosted = jnp.where((row_index == 0) | (row_index == PRIOR_ROWS - 1), 3, jnp.repeat(tier_draw, OLD_DEV, total_repeat_length=PRIOR_ROWS))
    affinity_grades = boosted.astype(jnp.int32) * PRIOR_ROWS + ranking
    selected_ones = jnp.argsort(-affinity_grades, stable=True)[:SURVIVING_LOT]
    return jax.random.permutation(shuffle_key, selected_ones).astype(jnp.int32)


def draw_retained_turned_probes(key, part):
    base_key = jax.random.fold_in(key, 0)
    full_shape = (PRIOR_ROWS, PLACES_CEILING, RECALL_STREAMS * FOCUS_BREADTHS)
    base = jnp.clip(jax.random.normal(base_key, full_shape, jnp.float32), -6.0, 6.0)
    return base.astype(jnp.bfloat16)


def touch_ends(result, stream_key, least, high):
    index_at = [jax.random.randint(jax.random.fold_in(stream_key, axis), (), 0, length) for axis, length in enumerate(result.shape)]
    main_axis = result.shape.index(max(result.shape))
    neighbour = index_at[:main_axis] + [(index_at[main_axis] + 1) % result.shape[main_axis]] + index_at[main_axis + 1:]
    return result.at[tuple(index_at)].set(least).at[tuple(neighbour)].set(high)


def steps_of(own_key, dims, cuts, smallest, high):
    factor_of, own = 1.0, jax.random.fold_in(own_key, 6)
    for dim, parts in cuts:
        heights = jnp.exp(jax.random.uniform(jax.random.fold_in(own, dim), (parts,), jnp.float32, smallest / len(cuts), high / len(cuts)))
        factor_of = factor_of * jnp.repeat(heights, dims[dim] // parts).reshape([-1 if axis == dim else 1 for axis in range(len(dims))])
    return factor_of


def noise(key, dims, width, reach, cuts=(), held_as=jnp.bfloat16):
    factor_of = steps_of(key, dims, cuts, -0.22, 0.18) if cuts else 1.0
    values = jax.random.normal(key, dims, jnp.float32) * width * factor_of
    return jnp.minimum(jnp.maximum(values, -reach), reach).astype(held_as)


def setup_inputs(seed: int = 0, part: int = 0) -> dict:
    splits = jax.random.split(jax.random.key(seed), 8)
    own_keys = jax.random.split(jax.random.fold_in(splits[7], part), 8)
    rescaled_signals = noise(own_keys[0], (EMIT_ITERATIONS, SURVIVING_LOT, HIDDEN_BREADTHS), 1.0, 6.0, ((1, 2),))
    linear_matrix = noise(splits[1], (HIDDEN_BREADTHS, RECALL_STREAMS * (ASKERS_SHARING + 2) * FOCUS_BREADTHS), HIDDEN_BREADTHS ** -0.5, 0.0625, ((0, 2), (1, 8)))
    linear_offset = noise(splits[2], (RECALL_STREAMS * (ASKERS_SHARING + 2) * FOCUS_BREADTHS,), 1.0, 4.0, ((0, 8),))
    retained_turned_probes = draw_retained_turned_probes(jax.random.fold_in(jax.random.fold_in(splits[7], part), 71), part)
    retained_payload = noise(own_keys[4], (PRIOR_ROWS, PLACES_CEILING, RECALL_STREAMS * FOCUS_BREADTHS), 1.0, 6.0, ((0, 16),))
    filled_extents = touch_ends(jax.random.randint(own_keys[5], (PRIOR_ROWS,), 1, PLACES_CEILING + 1), jax.random.fold_in(own_keys[5], 1), 1, PLACES_CEILING).astype(jnp.int32)
    prior_owner_lines = draw_prior_owner_lines(jax.random.fold_in(jax.random.fold_in(splits[7], part), 71), part)
    return {"rescaled_signals": rescaled_signals, "linear_matrix": linear_matrix, "linear_offset": linear_offset, "retained_turned_probes": retained_turned_probes, "retained_payload": retained_payload, "filled_extents": filled_extents, "prior_owner_lines": prior_owner_lines}


ROPE_BASE = 1000000.0


def rope_angles(positions, head_dim):
    frequency = ROPE_BASE ** (-jnp.arange(0, head_dim, 2, dtype=jnp.float32) / head_dim)
    angles = positions.astype(jnp.float32)[..., None] * frequency
    cosine = jnp.cos(angles)
    sine_table = jnp.sin(angles)
    return jnp.concatenate([cosine, cosine], -1), jnp.concatenate([sine_table, sine_table], -1)


def rotate(values, cosine, sine_table):
    front_half, back_half = jnp.split(values, 2, axis=-1)
    return values * cosine + jnp.concatenate([-back_half, front_half], -1) * sine_table


def reference(rescaled_signals, linear_matrix, linear_offset, retained_turned_probes, retained_payload, filled_extents, prior_owner_lines):
    unrolled_array = rescaled_signals.reshape(EMIT_ITERATIONS * SURVIVING_LOT, HIDDEN_BREADTHS)
    transformed_records = jnp.dot(unrolled_array, linear_matrix, preferred_element_type=jnp.float32) + linear_offset.astype(jnp.float32)
    compacted_records = transformed_records.astype(jnp.bfloat16).reshape(EMIT_ITERATIONS, SURVIVING_LOT, RECALL_STREAMS, ASKERS_SHARING + 2, FOCUS_BREADTHS)
    queries = compacted_records[:, :, :, :ASKERS_SHARING, :]
    new_keys = compacted_records[:, :, :, ASKERS_SHARING, :]
    new_values = compacted_records[:, :, :, ASKERS_SHARING + 1, :]
    sequence_extent = jnp.take(filled_extents, prior_owner_lines, axis=0).astype(jnp.int32)
    positions = sequence_extent[None, :] + jnp.arange(EMIT_ITERATIONS, dtype=jnp.int32)[:, None]
    cosine, sine_table = rope_angles(positions, FOCUS_BREADTHS)
    q_rot = rotate(queries.astype(jnp.float32), cosine[:, :, None, None, :], sine_table[:, :, None, None, :]).astype(jnp.bfloat16)
    k_rot = rotate(new_keys.astype(jnp.float32), cosine[:, :, None, :], sine_table[:, :, None, :]).astype(jnp.bfloat16)
    chance_starters = jnp.take(retained_turned_probes, prior_owner_lines, axis=0).reshape(SURVIVING_LOT, PLACES_CEILING, RECALL_STREAMS, FOCUS_BREADTHS).astype(jnp.float32)
    stashed_recall = jnp.take(retained_payload, prior_owner_lines, axis=0).reshape(SURVIVING_LOT, PLACES_CEILING, RECALL_STREAMS, FOCUS_BREADTHS).astype(jnp.float32)
    q_wide = q_rot.astype(jnp.float32)
    scale = FOCUS_BREADTHS ** -0.5
    cache_scores = jnp.einsum("srkgd,rlkd->srkgl", q_wide, chance_starters) * scale
    valid = jnp.arange(PLACES_CEILING, dtype=jnp.int32)[None, :] < sequence_extent[:, None]
    cache_scores = jnp.where(valid[None, :, None, None, :], cache_scores, -1e30)
    new_scores = jnp.einsum("srkgd,trkd->srkgt", q_wide, k_rot.astype(jnp.float32)) * scale
    causal = jnp.arange(EMIT_ITERATIONS)[:, None] >= jnp.arange(EMIT_ITERATIONS)[None, :]
    new_scores = jnp.where(causal[:, None, None, None, :], new_scores, -1e30)
    joined = jnp.concatenate([cache_scores, new_scores], -1)
    top_score = jnp.max(joined, axis=-1, keepdims=True)
    expo = jnp.exp(joined - top_score)
    weights = (expo / jnp.sum(expo, axis=-1, keepdims=True)).astype(jnp.bfloat16).astype(jnp.float32)
    blended_result = jnp.einsum("srkgl,rlkd->srkgd", weights[..., :PLACES_CEILING], stashed_recall)
    blended_result = blended_result + jnp.einsum("srkgt,trkd->srkgd", weights[..., PLACES_CEILING:], new_values.astype(jnp.float32))
    return blended_result.astype(jnp.bfloat16).reshape(EMIT_ITERATIONS, SURVIVING_LOT, ASKING_STREAMS * FOCUS_BREADTHS)
```

```python
import functools

import jax
import jax.numpy as jnp
from jax import lax
from jax.experimental import pallas as pl
from jax.experimental.pallas import tpu as pltpu
from jax.sharding import PartitionSpec as P

HEAD = 128
SHARING = 8
ROPE_BASE = 1000000.0
SWAP = ((0, 1), (1, 0))
CHUNKS = ((4, 8), (0, 4))


def rope_tables(positions):
    frequency = ROPE_BASE ** (-jnp.arange(0, HEAD, 2, dtype=jnp.float32) / HEAD)
    angles = positions.astype(jnp.float32)[..., None] * frequency
    cosine = jnp.cos(angles)
    sine = jnp.sin(angles)
    return jnp.concatenate([cosine, cosine], -1), jnp.concatenate([-sine, sine], -1)


def attention_kernel(heads, rows, fill_ref, cos_ref, sin_ref, q_ref, k_new_ref, v_new_ref,
                     k_ref, v_ref, out_ref, q_rot, k_rot, v_new, blended):
    scale = HEAD ** (-0.5)
    width = 2 * heads

    def turned(values, step):
        values = values.astype(jnp.float32)
        turn = values * cos_ref[step] + pltpu.roll(values, HEAD // 2, 1) * sin_ref[step]
        return turn.astype(jnp.bfloat16).astype(jnp.float32)

    for step in range(2):
        for head in range(heads):
            block = q_ref[step, 0, :, head * HEAD:(head + 1) * HEAD]
            q_rot[pl.ds((step * heads + head) * rows, rows), :] = turned(block, step)
        k_rot[pl.ds(step * rows, rows), :] = turned(k_new_ref[step, 0], step)
        v_new[pl.ds(step * rows, rows), :] = v_new_ref[step, 0].astype(jnp.float32)

    place = lax.broadcasted_iota(jnp.int32, (width, HEAD), 1)
    second = lax.broadcasted_iota(jnp.int32, (width, 1), 0) >= heads

    def group(base, carry):
        for inner in range(8):
            row = base * 8 + inner
            q = q_rot[pl.ds(row, width, stride=rows), :]
            scores = lax.dot_general(
                q.astype(jnp.bfloat16), k_ref[row], (((1,), (1,)), ((), ())),
                preferred_element_type=jnp.float32,
            ) * scale
            scores = jnp.where(place < fill_ref[row], scores, -1e30)
            first_new = jnp.sum(q * k_rot[pl.ds(row, 1), :], -1, keepdims=True) * scale
            second_new = jnp.sum(q * k_rot[pl.ds(rows + row, 1), :], -1, keepdims=True) * scale
            second_new = jnp.where(second, second_new, -1e30)
            top = jnp.maximum(
                jnp.max(scores, -1, keepdims=True), jnp.maximum(first_new, second_new)
            )
            expo = jnp.exp(scores - top)
            expo_first = jnp.exp(first_new - top)
            expo_second = jnp.exp(second_new - top)
            total = jnp.sum(expo, -1, keepdims=True) + expo_first + expo_second
            share = 1.0 / total
            mixed = jnp.dot(
                (expo * share).astype(jnp.bfloat16), v_ref[row],
                preferred_element_type=jnp.float32,
            )
            w_first = (expo_first * share).astype(jnp.bfloat16).astype(jnp.float32)
            w_second = (expo_second * share).astype(jnp.bfloat16).astype(jnp.float32)
            mixed = mixed + w_first * v_new[pl.ds(row, 1), :]
            mixed = mixed + w_second * v_new[pl.ds(rows + row, 1), :]
            blended[pl.ds(row, width, stride=rows), :] = mixed
        return carry

    lax.fori_loop(0, rows // 8, group, 0)
    for step in range(2):
        for head in range(heads):
            done = blended[pl.ds((step * heads + head) * rows, rows), :].astype(jnp.bfloat16)
            for pair in range(2):
                out_ref[pair, 0, step, :, head * HEAD:(head + 1) * HEAD] = done


def attend(fill, cosine, sine, queries, q_at, new, k_at, keys, values, heads):
    _, n_tp, rows, _ = queries.shape
    places = keys.shape[1]
    width = 2 * heads * rows
    table = pl.BlockSpec((2, rows, HEAD), lambda t, f: (0, 0, 0))
    cache = pl.BlockSpec((rows, places, HEAD), lambda t, f: (0, 0, t))
    return pl.pallas_call(
        functools.partial(attention_kernel, heads, rows),
        out_shape=jax.ShapeDtypeStruct((2, n_tp, 2, rows, heads * HEAD), jnp.bfloat16),
        grid_spec=pltpu.PrefetchScalarGridSpec(
            num_scalar_prefetch=1,
            grid=(n_tp,),
            in_specs=[
                table,
                table,
                pl.BlockSpec((2, 1, rows, heads * HEAD), lambda t, f: (0, t, 0, q_at)),
                pl.BlockSpec((2, 1, rows, HEAD), lambda t, f: (0, t, 0, k_at)),
                pl.BlockSpec((2, 1, rows, HEAD), lambda t, f: (0, t, 0, k_at + 1)),
                cache,
                cache,
            ],
            out_specs=pl.BlockSpec((2, 1, 2, rows, heads * HEAD), lambda t, f: (0, t, 0, 0, 0)),
            scratch_shapes=[
                pltpu.VMEM((width, HEAD), jnp.float32),
                pltpu.VMEM((2 * rows, HEAD), jnp.float32),
                pltpu.VMEM((2 * rows, HEAD), jnp.float32),
                pltpu.VMEM((width, HEAD), jnp.float32),
            ],
        ),
        compiler_params=pltpu.CompilerParams(vmem_limit_bytes=32 << 20),
        cost_estimate=pl.CostEstimate(
            flops=4 * width * n_tp * places * HEAD,
            transcendentals=width * n_tp * places,
            bytes_accessed=4 * rows * places * n_tp * HEAD,
        ),
    )(
        fill, cosine, sine, queries, new, new,
        pltpu.with_memory_space_constraint(keys, pltpu.HBM),
        pltpu.with_memory_space_constraint(values, pltpu.HBM),
    )


def per_device(signals, matrix, offset, cached_keys, cached_values, fill, lines):
    n_pair, n_tp, n_grp = (lax.axis_size(a) for a in ("pair", "tp", "grp"))
    pair, tp, grp = (lax.axis_index(a) for a in ("pair", "tp", "grp"))
    share, features = signals.shape[1:]
    half = matrix.shape[0]
    rows = fill.shape[0]
    owners = n_pair * n_tp

    n_y = n_tp // 2
    y = tp // 2
    piece = share // n_y
    depth = half // n_grp
    mine = lax.dynamic_index_in_dim(signals, pair, 0, keepdims=False)
    theirs = lax.dynamic_index_in_dim(signals, 1 - pair, 0, keepdims=False)
    sent = lax.dynamic_slice_in_dim(theirs, y * piece, piece)
    sent_first, sent_second = sent[:piece // 2], sent[piece // 2:]
    slab = lax.dynamic_slice_in_dim(matrix, grp * depth, depth)
    spans = [
        (start * HEAD, (stop + 2 if stop == SHARING else stop) * HEAD) for start, stop in CHUNKS
    ]
    up = [(2 * a + h, 2 * ((a + 1) % n_y) + h) for a in range(n_y) for h in range(2)]
    down = [(d, s) for s, d in up]

    def after(value, *earlier):
        return lax.optimization_barrier((value, *earlier))[0]

    near_first = lax.ppermute(sent_first, "pair", SWAP)
    moved = lax.ppermute(slab[:, slice(*spans[0])], "pair", SWAP)
    far = [lax.all_gather(moved, "grp", axis=0, tiled=True)]
    near_second = lax.ppermute(after(sent_second, near_first, moved), "pair", SWAP)
    for span in spans[1:]:
        moved = lax.ppermute(after(slab[:, slice(*span)], near_second, moved), "pair", SWAP)
        far.append(lax.all_gather(after(moved, far[-1]), "grp", axis=0, tiled=True))
    below_first = lax.ppermute(near_first, "tp", up)
    above_first = lax.ppermute(near_first, "tp", down)
    below_second = lax.ppermute(near_second, "tp", up)
    above_second = lax.ppermute(near_second, "tp", down)
    far_first = lax.ppermute(below_first, "tp", up)
    far_second = lax.ppermute(above_second, "tp", down)
    theirs = jnp.concatenate(
        [near_first, near_second, below_first, below_second, above_first, above_second,
         far_first, far_second], 0
    )
    listed = [lax.dynamic_slice_in_dim(lines, pair * share, share)] + [
        lax.dynamic_slice_in_dim(
            lines, (1 - pair) * share + (y + turn) % n_y * piece, piece
        )
        for turn in (0, n_y - 1, 1, 2)
    ]
    listed = jnp.concatenate(listed)
    pack = (
        jnp.arange(owners * rows, dtype=jnp.int32)[:, None] == listed[None, :]
    ).astype(jnp.bfloat16)

    def split(block):
        return (
            lax.dynamic_slice_in_dim(block, pair * half, half, 1),
            lax.dynamic_slice_in_dim(block, (1 - pair) * half, half, 1),
        )

    mine_near, mine_far = split(mine)
    theirs_near, theirs_far = split(theirs)
    all_far = jnp.concatenate([mine_far, theirs_far], 0)
    f32 = functools.partial(jnp.dot, preferred_element_type=jnp.float32)
    mine_sum = f32(mine_near, matrix)
    theirs_sum = f32(theirs_near, matrix)
    partial = jnp.concatenate([mine_sum, theirs_sum], 0) + offset.astype(jnp.float32)

    positions = fill[None, :] + jnp.arange(2, dtype=jnp.int32)[:, None]
    cosine, sine = rope_tables(positions)
    own = lax.dynamic_slice_in_dim(lines, pair * share, share)
    pick = (
        own[:, None] == jnp.arange(owners * rows, dtype=jnp.int32)[None, :]
    ).astype(jnp.bfloat16).reshape(share, owners, rows)

    outs, new, k_at = {}, None, None
    for (start, stop), remote in zip(CHUNKS, far):
        end = stop + 2 if stop == SHARING else stop
        projected = partial[:, start * HEAD:end * HEAD] + f32(all_far, remote)
        packed = f32(pack, projected.astype(jnp.bfloat16)).astype(jnp.bfloat16)
        packed = packed.reshape(owners, rows, (end - start) * HEAD)
        arrived = lax.all_to_all(
            packed, ("pair", "tp"), split_axis=0, concat_axis=0, tiled=True
        ).reshape(n_pair, n_tp, rows, (end - start) * HEAD)
        if new is None:
            new, k_at = arrived, stop - start
        attended = attend(
            fill, cosine, sine, arrived, 0, new, k_at, cached_keys, cached_values, stop - start
        )
        back = lax.all_to_all(
            attended.reshape(owners, 2, rows, (stop - start) * HEAD),
            ("pair", "tp"), split_axis=0, concat_axis=0, tiled=True,
        )
        outs[start] = jnp.einsum(
            "rgj,gsjn->srn", pick, back, preferred_element_type=jnp.float32
        ).astype(jnp.bfloat16)
    return jnp.concatenate([outs[k] for k in sorted(outs)], -1)


def solution(mesh):
    in_specs = (
        P(None, ("grp", "pair"), None),
        P("pair", "tp"),
        P("tp"),
        P(("grp", "pair", "tp"), None, None),
        P(("grp", "pair", "tp"), None, None),
        P(("grp", "pair", "tp")),
        P("grp"),
    )
    out_specs = P(None, ("grp", "pair"), "tp")
    return jax.shard_map(
        per_device, mesh=mesh, in_specs=in_specs, out_specs=out_specs, check_vma=False
    )
```

```python
import functools

import jax
import jax.numpy as jnp
from jax import lax
from jax.experimental import pallas as pl
from jax.experimental.pallas import tpu as pltpu
from jax.sharding import PartitionSpec as P

HEAD = 128
SHARING = 8
ROPE_BASE = 1000000.0
SWAP = ((0, 1), (1, 0))
CHUNKS = ((0, 4), (4, 8))
ROW_BLOCK = 8
DEPTH_BLOCK = 1024
NT = (((1,), (1,)), ((), ()))


def in_hbm(value):
    return pltpu.with_memory_space_constraint(value, pltpu.HBM)


def rope_tables(positions):
    frequency = ROPE_BASE ** (-jnp.arange(0, HEAD, 2, dtype=jnp.float32) / HEAD)
    angles = positions.astype(jnp.float32)[..., None] * frequency
    cosine = jnp.cos(angles)
    sine = jnp.sin(angles)
    return jnp.concatenate([cosine, cosine], -1), jnp.concatenate([-sine, sine], -1)


def project_kernel(owners, rows, side_ref, x_ref, w_ref, partial_ref, pack_ref, out_ref, total):
    k = pl.program_id(0)
    product = jnp.dot(x_ref[...], w_ref[...], preferred_element_type=jnp.float32)

    @pl.when(k == 0)
    def _():
        total[...] = partial_ref[...] + product

    @pl.when(k > 0)
    def _():
        total[...] += product

    @pl.when(k == pl.num_programs(0) - 1)
    def _():
        share = pack_ref.shape[1]
        for step in range(2):
            rounded = total[pl.ds(step * share, share), :].astype(jnp.bfloat16)
            packed = jnp.dot(pack_ref[...], rounded, preferred_element_type=jnp.float32)
            for owner in range(owners):
                block = packed[owner * rows:(owner + 1) * rows]
                out_ref[owner, step] = block.astype(jnp.bfloat16)


def project(side, signals, matrix, partial, at, pack, owners):
    lines, _ = signals.shape
    depth, columns = matrix.shape
    slots, share = pack.shape
    rows = slots // owners
    steps = depth // DEPTH_BLOCK
    return pl.pallas_call(
        functools.partial(project_kernel, owners, rows),
        out_shape=pltpu.HBM((owners, 2, rows, columns), jnp.bfloat16),
        grid_spec=pltpu.PrefetchScalarGridSpec(
            num_scalar_prefetch=1,
            grid=(steps,),
            in_specs=[
                pl.BlockSpec((lines, DEPTH_BLOCK), lambda k, s: (0, s[0] * steps + k)),
                pl.BlockSpec((DEPTH_BLOCK, columns), lambda k, s: (k, 0)),
                pl.BlockSpec((lines, columns), lambda k, s: (0, at)),
                pl.BlockSpec((slots, share), lambda k, s: (0, 0)),
            ],
            out_specs=pl.BlockSpec((owners, 2, rows, columns), lambda k, s: (0, 0, 0, 0)),
            scratch_shapes=[pltpu.VMEM((lines, columns), jnp.float32)],
        ),
        compiler_params=pltpu.CompilerParams(vmem_limit_bytes=32 << 20),
        cost_estimate=pl.CostEstimate(
            flops=2 * lines * depth * columns,
            transcendentals=0,
            bytes_accessed=2 * (lines + columns) * depth,
        ),
    )(side, in_hbm(signals), in_hbm(matrix), partial, pack)


def attention_kernel(heads, fill_ref, cos_ref, sin_ref, q_ref, new_ref, k_ref, v_ref, out_ref,
                     q_rot, k_rot, v_new, cached_scores, new_scores, blended):
    n_tp = q_ref.shape[1]
    block = ROW_BLOCK
    scale = HEAD ** (-0.5)
    width = 2 * heads
    first = pl.program_id(0) * block
    size = block * width

    def both(ref, t, step, start):
        lanes = slice(start, start + HEAD)
        return ref[0, t, step, :, lanes].astype(jnp.float32) + ref[1, t, step, :, lanes].astype(jnp.float32)

    def turned(values, step):
        turn = values * cos_ref[step] + pltpu.roll(values, HEAD // 2, 1) * sin_ref[step]
        return turn.astype(jnp.bfloat16).astype(jnp.float32)

    place = lax.broadcasted_iota(jnp.int32, (width, HEAD), 1)
    line = lax.broadcasted_iota(jnp.int32, (size, 2 * block), 0)
    column = lax.broadcasted_iota(jnp.int32, (size, 2 * block), 1)
    seen = ((column % block) == (line // width)) & (
        (column < block) | (line % width >= heads)
    )
    filled = [place < fill_ref[first + i] for i in range(block)]

    for t in range(n_tp):
        for step in range(2):
            for head in range(heads):
                at = pl.ds(t * size + (step * heads + head) * block, block)
                q_rot[at, :] = turned(both(q_ref, t, step, head * HEAD), step)
            at = pl.ds(step * block, block)
            k_rot[t, at, :] = turned(both(new_ref, t, step, 0), step)
            v_new[t, at, :] = both(new_ref, t, step, HEAD)
    for t in range(n_tp):
        lanes = slice(t * HEAD, (t + 1) * HEAD)
        queries = [
            q_rot[pl.ds(t * size + i, width, stride=block), :].astype(jnp.bfloat16) for i in range(block)
        ]
        for i in range(block):
            scores = lax.dot_general(
                queries[i], k_ref[i, :, lanes], NT, preferred_element_type=jnp.float32
            ) * scale
            cached_scores[t, pl.ds(i * width, width), :] = jnp.where(filled[i], scores, -1e30)
        scores = lax.dot_general(
            jnp.concatenate(queries, 0), k_rot[t].astype(jnp.bfloat16), NT,
            preferred_element_type=jnp.float32,
        ) * scale
        new_scores[t] = jnp.where(seen, scores, -1e30)
    for t in range(n_tp):
        lanes = slice(t * HEAD, (t + 1) * HEAD)
        cached, new = cached_scores[t], new_scores[t]
        top = jnp.maximum(jnp.max(cached, -1, keepdims=True), jnp.max(new, -1, keepdims=True))
        cached, new = jnp.exp(cached - top), jnp.exp(new - top)
        share = 1.0 / (jnp.sum(cached, -1, keepdims=True) + jnp.sum(new, -1, keepdims=True))
        cached, new = (cached * share).astype(jnp.bfloat16), (new * share).astype(jnp.bfloat16)
        from_new = jnp.dot(new, v_new[t].astype(jnp.bfloat16), preferred_element_type=jnp.float32)
        for i in range(block):
            part = slice(i * width, (i + 1) * width)
            mixed = jnp.dot(cached[part], v_ref[i, :, lanes], preferred_element_type=jnp.float32)
            blended[pl.ds(t * size + i, width, stride=block), :] = mixed + from_new[part]
    for t in range(n_tp):
        for step in range(2):
            for head in range(heads):
                at = pl.ds(t * size + (step * heads + head) * block, block)
                done = blended[at, :].astype(jnp.bfloat16)
                for pair in range(2):
                    out_ref[pair, t, step, :, head * HEAD:(head + 1) * HEAD] = done


def attend(fill, cosine, sine, queries, new, keys, values, heads):
    _, n_tp, _, rows, _ = queries.shape
    places = keys.shape[1]
    block = ROW_BLOCK
    width = 2 * heads * block
    table = pl.BlockSpec((2, block, HEAD), lambda r, f: (0, r, 0))
    cache = pl.BlockSpec((block, places, n_tp * HEAD), lambda r, f: (r, 0, 0))

    def routed(columns):
        return pl.BlockSpec((2, n_tp, 2, block, columns), lambda r, f: (0, 0, 0, r, 0))

    return pl.pallas_call(
        functools.partial(attention_kernel, heads),
        out_shape=pltpu.HBM((2, n_tp, 2, rows, heads * HEAD), jnp.bfloat16),
        grid_spec=pltpu.PrefetchScalarGridSpec(
            num_scalar_prefetch=1,
            grid=(rows // block,),
            in_specs=[table, table, routed(heads * HEAD), routed(2 * HEAD), cache, cache],
            out_specs=routed(heads * HEAD),
            scratch_shapes=[
                pltpu.VMEM((n_tp * width, HEAD), jnp.float32),
                pltpu.VMEM((n_tp, 2 * block, HEAD), jnp.float32),
                pltpu.VMEM((n_tp, 2 * block, HEAD), jnp.float32),
                pltpu.VMEM((n_tp, width, HEAD), jnp.float32),
                pltpu.VMEM((n_tp, width, 2 * block), jnp.float32),
                pltpu.VMEM((n_tp * width, HEAD), jnp.float32),
            ],
        ),
        compiler_params=pltpu.CompilerParams(vmem_limit_bytes=32 << 20),
        cost_estimate=pl.CostEstimate(
            flops=8 * heads * rows * n_tp * places * HEAD,
            transcendentals=2 * heads * rows * n_tp * places,
            bytes_accessed=4 * rows * places * n_tp * HEAD,
        ),
    )(
        fill, cosine, sine, queries, new, in_hbm(keys), in_hbm(values)
    )


def unpack_kernel(owners, rows, pick_ref, back_ref, *refs):
    out_ref, gathered = refs[-2:]
    for owner in range(owners):
        gathered[pl.ds(owner * rows, rows), :] = back_ref[owner, 0].astype(jnp.float32)
    picked = jnp.dot(
        pick_ref[...], gathered[...].astype(jnp.bfloat16), preferred_element_type=jnp.float32
    )
    out_ref[0] = picked.astype(jnp.bfloat16)


def unpack(pick, back, at, columns, so_far):
    owners, _, rows, wide = back.shape
    share, slots = pick.shape
    before = [] if so_far is None else [so_far]
    return pl.pallas_call(
        functools.partial(unpack_kernel, owners, rows),
        out_shape=jax.ShapeDtypeStruct((2, share, columns), jnp.bfloat16),
        grid=(2,),
        in_specs=[
            pl.BlockSpec((share, slots), lambda s: (0, 0)),
            pl.BlockSpec((owners, 1, rows, wide), lambda s: (0, s, 0, 0)),
        ] + [pl.BlockSpec(memory_space=pl.ANY)] * len(before),
        out_specs=pl.BlockSpec((1, share, wide), lambda s: (s, 0, at)),
        scratch_shapes=[pltpu.VMEM((slots, wide), jnp.float32)],
        input_output_aliases={2: 0} if before else {},
        compiler_params=pltpu.CompilerParams(vmem_limit_bytes=32 << 20),
        cost_estimate=pl.CostEstimate(
            flops=4 * share * slots * wide, transcendentals=0, bytes_accessed=4 * slots * wide
        ),
    )(pick, back, *before)


def per_device(signals, matrix, offset, cached_keys, cached_values, fill, lines):
    n_pair, n_tp, n_grp = (int(lax.axis_size(a)) for a in ("pair", "tp", "grp"))
    pair, grp = (lax.axis_index(a) for a in ("pair", "grp"))
    share, features = signals.shape[1:]
    half, columns = matrix.shape
    rows = fill.shape[0]
    owners = n_pair * n_tp
    depth = half // n_grp

    def after(value, *earlier):
        return lax.optimization_barrier((value, *earlier))[0]

    spans = [(SHARING * HEAD, columns)] + [(a * HEAD, b * HEAD) for a, b in CHUNKS]
    moved = []
    for start, stop in spans:
        slab = lax.dynamic_slice(matrix, (grp * depth, start), (depth, stop - start))
        moved.append(lax.ppermute(after(slab, *moved[1:]), "pair", SWAP))

    flat = signals.reshape(2 * share, features)
    near = lax.dynamic_slice_in_dim(flat, pair * half, half, 1)
    partial = jnp.dot(near, matrix, preferred_element_type=jnp.float32)
    partial = partial + offset.astype(jnp.float32)
    side = jnp.reshape(1 - pair, (1,)).astype(jnp.int32)

    own = lax.dynamic_slice_in_dim(lines, pair * share, share)
    slots = jnp.arange(owners * rows, dtype=jnp.int32)
    pack = (slots[:, None] == own[None, :]).astype(jnp.bfloat16)
    pick = (own[:, None] == slots[None, :]).astype(jnp.bfloat16)
    positions = fill[None, :] + jnp.arange(2, dtype=jnp.int32)[:, None]
    cosine, sine = rope_tables(positions)

    def exchange(blocks):
        return lax.all_to_all(blocks, ("pair", "tp"), split_axis=0, concat_axis=0, tiled=True)

    arrived, remote, earlier = [], None, [partial, pack, pick, cosine, sine]
    for (start, stop), slab in zip(spans, moved):
        ready = slab if remote is None else after(slab, remote, *earlier)
        if remote is not None:
            earlier = [project(side, flat, *last)]
            arrived.append(exchange(earlier[0]))
        remote = lax.all_gather(ready, "grp", axis=0, tiled=True)
        last = (remote, partial, start // (stop - start), pack, owners)
    arrived.append(exchange(project(side, flat, *last)))
    arrived = [
        block.reshape(n_pair, n_tp, 2, rows, stop - start)
        for block, (start, stop) in zip(arrived, spans)
    ]
    out = None
    for (start, stop), queries in zip(spans[1:], arrived[1:]):
        heads = (stop - start) // HEAD
        attended = attend(
            fill, cosine, sine, queries, arrived[0], cached_keys, cached_values, heads
        )
        back = exchange(attended.reshape(owners, 2, rows, stop - start))
        out = unpack(pick, back, start // (stop - start), SHARING * HEAD, out)
    return out


def solution(mesh):
    in_specs = (
        P(None, ("grp", "pair"), None),
        P("pair", "tp"),
        P("tp"),
        P(("grp", "pair", "tp"), None, None),
        P(("grp", "pair", "tp"), None, None),
        P(("grp", "pair", "tp")),
        P("grp"),
    )
    out_specs = P(None, ("grp", "pair"), "tp")
    return jax.shard_map(
        per_device, mesh=mesh, in_specs=in_specs, out_specs=out_specs, check_vma=False
    )
```

```python
import functools

import jax
import jax.numpy as jnp
from jax import lax
from jax.experimental import pallas as pl
from jax.experimental.pallas import tpu as pltpu
from jax.sharding import PartitionSpec as P

HEAD = 128
SHARING = 8
ROPE_BASE = 1000000.0
SWAP = ((0, 1), (1, 0))
CHUNKS = ((0, 4), (4, 8))
ROW_BLOCK = 8
NT = (((1,), (1,)), ((), ()))


def in_hbm(value):
    return pltpu.with_memory_space_constraint(value, pltpu.HBM)


def rope_tables(positions):
    frequency = ROPE_BASE ** (-jnp.arange(0, HEAD, 2, dtype=jnp.float32) / HEAD)
    angles = positions.astype(jnp.float32)[..., None] * frequency
    cosine = jnp.cos(angles)
    sine = jnp.sin(angles)
    return jnp.concatenate([cosine, cosine], -1), jnp.concatenate([-sine, sine], -1)


def project_kernel(columns, owners, rows, places_ref, x_ref, *refs):
    slabs = refs[:-6]
    partial_ref, pack_ref, out_ref, taken, total, arrived = refs[-6:]
    depth = slabs[0].shape[0]
    share = pack_ref.shape[1]
    copies = []
    for i in range(len(slabs)):
        first = pl.multiple_of(places_ref[i] * depth, depth)
        copies.append(
            pltpu.make_async_copy(x_ref.at[:, pl.ds(first, depth)], taken.at[i], arrived.at[i])
        )
        copies[i].start()
    for i, slab in enumerate(slabs):
        copies[i].wait()
        product = jnp.dot(taken[i], slab[...], preferred_element_type=jnp.float32)
        if i == 0:
            total[...] = partial_ref[:, slice(*columns)] + product
        else:
            total[...] += product
    for step in range(2):
        rounded = total[pl.ds(step * share, share), :].astype(jnp.bfloat16)
        packed = jnp.dot(pack_ref[...], rounded, preferred_element_type=jnp.float32)
        for owner in range(owners):
            block = packed[owner * rows:(owner + 1) * rows]
            out_ref[owner, step] = block.astype(jnp.bfloat16)


def project(places, signals, slabs, partial, columns, pack, owners):
    lines, _ = signals.shape
    depth, wide = slabs[0].shape
    slots, share = pack.shape
    rows = slots // owners
    local = pl.BlockSpec(memory_space=pltpu.VMEM)
    return pl.pallas_call(
        functools.partial(project_kernel, columns, owners, rows),
        out_shape=pltpu.HBM((owners, 2, rows, wide), jnp.bfloat16),
        grid_spec=pltpu.PrefetchScalarGridSpec(
            num_scalar_prefetch=1,
            grid=(1,),
            in_specs=[pl.BlockSpec(memory_space=pl.ANY)] + [local] * (len(slabs) + 2),
            out_specs=pl.BlockSpec((owners, 2, rows, wide), lambda k, s: (0, 0, 0, 0)),
            scratch_shapes=[
                pltpu.VMEM((len(slabs), lines, depth), jnp.bfloat16),
                pltpu.VMEM((lines, wide), jnp.float32),
                pltpu.SemaphoreType.DMA((len(slabs),)),
            ],
        ),
        compiler_params=pltpu.CompilerParams(vmem_limit_bytes=32 << 20),
        cost_estimate=pl.CostEstimate(
            flops=2 * lines * depth * len(slabs) * wide,
            transcendentals=0,
            bytes_accessed=2 * lines * depth * len(slabs),
        ),
    )(places, in_hbm(signals), *slabs, partial, pack)


def attention_kernel(heads, fill_ref, cos_ref, sin_ref, q_ref, new_ref, k_ref, v_ref, out_ref,
                     q_rot, k_rot, v_new, cached_scores, new_scores, blended):
    n_tp = q_ref.shape[1]
    block = ROW_BLOCK
    scale = HEAD ** (-0.5)
    width = 2 * heads
    first = pl.program_id(0) * block
    size = block * width

    def both(ref, t, step, start):
        lanes = slice(start, start + HEAD)
        return ref[0, t, step, :, lanes].astype(jnp.float32) + ref[1, t, step, :, lanes].astype(jnp.float32)

    def turned(values, step):
        turn = values * cos_ref[step] + pltpu.roll(values, HEAD // 2, 1) * sin_ref[step]
        return turn.astype(jnp.bfloat16).astype(jnp.float32)

    place = lax.broadcasted_iota(jnp.int32, (width, HEAD), 1)
    line = lax.broadcasted_iota(jnp.int32, (size, 2 * block), 0)
    column = lax.broadcasted_iota(jnp.int32, (size, 2 * block), 1)
    seen = ((column % block) == (line // width)) & (
        (column < block) | (line % width >= heads)
    )
    filled = [place < fill_ref[first + i] for i in range(block)]

    for t in range(n_tp):
        for step in range(2):
            for head in range(heads):
                at = pl.ds(t * size + (step * heads + head) * block, block)
                q_rot[at, :] = turned(both(q_ref, t, step, head * HEAD), step)
            at = pl.ds(step * block, block)
            k_rot[t, at, :] = turned(both(new_ref, t, step, 0), step)
            v_new[t, at, :] = both(new_ref, t, step, HEAD)
    for t in range(n_tp):
        lanes = slice(t * HEAD, (t + 1) * HEAD)
        queries = [
            q_rot[pl.ds(t * size + i, width, stride=block), :].astype(jnp.bfloat16) for i in range(block)
        ]
        for i in range(block):
            scores = lax.dot_general(
                queries[i], k_ref[i, :, lanes], NT, preferred_element_type=jnp.float32
            ) * scale
            cached_scores[t, pl.ds(i * width, width), :] = jnp.where(filled[i], scores, -1e30)
        scores = lax.dot_general(
            jnp.concatenate(queries, 0), k_rot[t].astype(jnp.bfloat16), NT,
            preferred_element_type=jnp.float32,
        ) * scale
        new_scores[t] = jnp.where(seen, scores, -1e30)
    for t in range(n_tp):
        lanes = slice(t * HEAD, (t + 1) * HEAD)
        cached, new = cached_scores[t], new_scores[t]
        top = jnp.maximum(jnp.max(cached, -1, keepdims=True), jnp.max(new, -1, keepdims=True))
        cached, new = jnp.exp(cached - top), jnp.exp(new - top)
        share = 1.0 / (jnp.sum(cached, -1, keepdims=True) + jnp.sum(new, -1, keepdims=True))
        cached, new = (cached * share).astype(jnp.bfloat16), (new * share).astype(jnp.bfloat16)
        from_new = jnp.dot(new, v_new[t].astype(jnp.bfloat16), preferred_element_type=jnp.float32)
        for i in range(block):
            part = slice(i * width, (i + 1) * width)
            mixed = jnp.dot(cached[part], v_ref[i, :, lanes], preferred_element_type=jnp.float32)
            blended[pl.ds(t * size + i, width, stride=block), :] = mixed + from_new[part]
    for t in range(n_tp):
        for step in range(2):
            for head in range(heads):
                at = pl.ds(t * size + (step * heads + head) * block, block)
                done = blended[at, :].astype(jnp.bfloat16)
                for pair in range(2):
                    out_ref[pair, t, step, :, head * HEAD:(head + 1) * HEAD] = done


def attend(fill, cosine, sine, queries, new, keys, values, heads):
    _, n_tp, _, rows, _ = queries.shape
    places = keys.shape[1]
    block = ROW_BLOCK
    width = 2 * heads * block
    table = pl.BlockSpec((2, block, HEAD), lambda r, f: (0, r, 0))
    cache = pl.BlockSpec((block, places, n_tp * HEAD), lambda r, f: (r, 0, 0))

    def routed(columns):
        return pl.BlockSpec((2, n_tp, 2, block, columns), lambda r, f: (0, 0, 0, r, 0))

    return pl.pallas_call(
        functools.partial(attention_kernel, heads),
        out_shape=pltpu.HBM((2, n_tp, 2, rows, heads * HEAD), jnp.bfloat16),
        grid_spec=pltpu.PrefetchScalarGridSpec(
            num_scalar_prefetch=1,
            grid=(rows // block,),
            in_specs=[table, table, routed(heads * HEAD), routed(2 * HEAD), cache, cache],
            out_specs=routed(heads * HEAD),
            scratch_shapes=[
                pltpu.VMEM((n_tp * width, HEAD), jnp.float32),
                pltpu.VMEM((n_tp, 2 * block, HEAD), jnp.float32),
                pltpu.VMEM((n_tp, 2 * block, HEAD), jnp.float32),
                pltpu.VMEM((n_tp, width, HEAD), jnp.float32),
                pltpu.VMEM((n_tp, width, 2 * block), jnp.float32),
                pltpu.VMEM((n_tp * width, HEAD), jnp.float32),
            ],
        ),
        compiler_params=pltpu.CompilerParams(vmem_limit_bytes=32 << 20),
        cost_estimate=pl.CostEstimate(
            flops=8 * heads * rows * n_tp * places * HEAD,
            transcendentals=2 * heads * rows * n_tp * places,
            bytes_accessed=4 * rows * places * n_tp * HEAD,
        ),
    )(
        fill, cosine, sine, queries, new, in_hbm(keys), in_hbm(values)
    )


def unpack_kernel(owners, rows, pick_ref, back_ref, *refs):
    out_ref, gathered = refs[-2:]
    for owner in range(owners):
        gathered[pl.ds(owner * rows, rows), :] = back_ref[owner, 0].astype(jnp.float32)
    picked = jnp.dot(
        pick_ref[...], gathered[...].astype(jnp.bfloat16), preferred_element_type=jnp.float32
    )
    out_ref[0] = picked.astype(jnp.bfloat16)


def unpack(pick, back, at, columns, so_far):
    owners, _, rows, wide = back.shape
    share, slots = pick.shape
    before = [] if so_far is None else [so_far]
    return pl.pallas_call(
        functools.partial(unpack_kernel, owners, rows),
        out_shape=jax.ShapeDtypeStruct((2, share, columns), jnp.bfloat16),
        grid=(2,),
        in_specs=[
            pl.BlockSpec((share, slots), lambda s: (0, 0)),
            pl.BlockSpec((owners, 1, rows, wide), lambda s: (0, s, 0, 0)),
        ] + [pl.BlockSpec(memory_space=pl.ANY)] * len(before),
        out_specs=pl.BlockSpec((1, share, wide), lambda s: (s, 0, at)),
        scratch_shapes=[pltpu.VMEM((slots, wide), jnp.float32)],
        input_output_aliases={2: 0} if before else {},
        compiler_params=pltpu.CompilerParams(vmem_limit_bytes=32 << 20),
        cost_estimate=pl.CostEstimate(
            flops=4 * share * slots * wide, transcendentals=0, bytes_accessed=4 * slots * wide
        ),
    )(pick, back, *before)


def per_device(signals, matrix, offset, cached_keys, cached_values, fill, lines):
    n_pair, n_tp, n_grp = (int(lax.axis_size(a)) for a in ("pair", "tp", "grp"))
    pair, grp = (lax.axis_index(a) for a in ("pair", "grp"))
    share, features = signals.shape[1:]
    half, columns = matrix.shape
    rows = fill.shape[0]
    owners = n_pair * n_tp
    depth = half // n_grp

    def after(value, *earlier):
        return lax.optimization_barrier((value, *earlier))[0]

    flat = signals.reshape(2 * share, features)
    own = lax.dynamic_slice_in_dim(lines, pair * share, share)
    slots = jnp.arange(owners * rows, dtype=jnp.int32)
    pack = (slots[:, None] == own[None, :]).astype(jnp.bfloat16)
    pick = (own[:, None] == slots[None, :]).astype(jnp.bfloat16)
    positions = fill[None, :] + jnp.arange(2, dtype=jnp.int32)[:, None]
    cosine, sine = rope_tables(positions)

    def exchange(blocks):
        return lax.all_to_all(blocks, ("pair", "tp"), split_axis=0, concat_axis=0, tiled=True)

    spans = [(SHARING * HEAD, columns)] + [(a * HEAD, b * HEAD) for a, b in CHUNKS]
    n_z = n_grp // 2
    up = [(2 * a + c, 2 * ((a + 1) % n_z) + c) for a in range(n_z) for c in range(2)]
    down = [(d, s) for s, d in up]
    twin = [(2 * a + c, 2 * a + 1 - c) for a in range(n_z) for c in range(2)]
    z, core = grp // 2, grp % 2
    turns = (0, n_z - 1, 1, 2)
    places = (1 - pair) * n_grp + jnp.stack(
        [(z + turn) % n_z * 2 + core for turn in turns]
        + [(z + turn) % n_z * 2 + 1 - core for turn in turns]
    )
    places = places.astype(jnp.int32)

    first = []
    for start, stop in spans:
        slab = lax.dynamic_slice(matrix, (grp * depth, start), (depth, stop - start))
        first.append(lax.ppermute(after(slab, *first[-1:]), "pair", SWAP))
    near = lax.dynamic_slice_in_dim(flat, pair * half, half, 1)
    partial = jnp.dot(near, matrix, preferred_element_type=jnp.float32)
    partial = partial + offset.astype(jnp.float32)

    arrived, ahead = [], []
    for number, ((start, stop), slab) in enumerate(zip(spans, first)):
        slab = after(slab, *ahead)
        below = lax.ppermute(slab, "grp", up)
        above = lax.ppermute(slab, "grp", down)
        ahead = [below, above]
        if number % 2:
            opposite = lax.ppermute(above, "grp", down)
        else:
            opposite = lax.ppermute(below, "grp", up)
        if number == 1:
            opposite = after(opposite, arrived[0])
        held = [slab, below, above, opposite]
        held += [lax.ppermute(piece, "grp", twin) for piece in held]
        packed = project(places, flat, held, partial, (start, stop), pack, owners)
        arrived.append(exchange(packed).reshape(n_pair, n_tp, 2, rows, stop - start))
    out = None
    for (start, stop), queries in zip(spans[1:], arrived[1:]):
        heads = (stop - start) // HEAD
        attended = attend(
            fill, cosine, sine, queries, arrived[0], cached_keys, cached_values, heads
        )
        back = exchange(attended.reshape(owners, 2, rows, stop - start))
        out = unpack(pick, back, start // (stop - start), SHARING * HEAD, out)
    return out


def solution(mesh):
    in_specs = (
        P(None, ("grp", "pair"), None),
        P("pair", "tp"),
        P("tp"),
        P(("grp", "pair", "tp"), None, None),
        P(("grp", "pair", "tp"), None, None),
        P(("grp", "pair", "tp")),
        P("grp"),
    )
    out_specs = P(None, ("grp", "pair"), "tp")
    return jax.shard_map(
        per_device, mesh=mesh, in_specs=in_specs, out_specs=out_specs, check_vma=False
    )
```

```python
import functools

import jax
import jax.numpy as jnp
from jax import lax
from jax.experimental import pallas as pl
from jax.experimental.pallas import tpu as pltpu
from jax.sharding import PartitionSpec as P

HEAD = 128
SHARING = 8
ROPE_BASE = 1000000.0
SWAP = ((0, 1), (1, 0))
CHUNKS = ((4, 8), (0, 4))
ROW_BLOCK = 8
NT = (((1,), (1,)), ((), ()))


def in_hbm(value):
    return pltpu.with_memory_space_constraint(value, pltpu.HBM)


def rope_tables(positions):
    frequency = ROPE_BASE ** (-jnp.arange(0, HEAD, 2, dtype=jnp.float32) / HEAD)
    angles = positions.astype(jnp.float32)[..., None] * frequency
    cosine = jnp.cos(angles)
    sine = jnp.sin(angles)
    return jnp.concatenate([cosine, cosine], -1), jnp.concatenate([-sine, sine], -1)


def project_kernel(owners, rows, places_ref, x_ref, *refs):
    slabs = refs[:-6]
    partial_ref, pack_ref, out_ref, taken, total, arrived = refs[-6:]
    depth = slabs[0].shape[0]
    share = pack_ref.shape[1]
    copies = []
    for i in range(len(slabs)):
        first = pl.multiple_of(places_ref[i] * depth, depth)
        copies.append(
            pltpu.make_async_copy(x_ref.at[:, pl.ds(first, depth)], taken.at[i], arrived.at[i])
        )
        copies[i].start()
    for i, slab in enumerate(slabs):
        copies[i].wait()
        product = jnp.dot(taken[i], slab[...], preferred_element_type=jnp.float32)
        if i == 0:
            total[...] = partial_ref[...] + product
        else:
            total[...] += product
    for step in range(2):
        rounded = total[pl.ds(step * share, share), :].astype(jnp.bfloat16)
        packed = jnp.dot(pack_ref[...], rounded, preferred_element_type=jnp.float32)
        for owner in range(owners):
            block = packed[owner * rows:(owner + 1) * rows]
            out_ref[owner, step] = block.astype(jnp.bfloat16)


def project(places, signals, slabs, partial, pack, owners):
    lines, _ = signals.shape
    depth, wide = slabs[0].shape
    slots, share = pack.shape
    rows = slots // owners
    local = pl.BlockSpec(memory_space=pltpu.VMEM)
    return pl.pallas_call(
        functools.partial(project_kernel, owners, rows),
        out_shape=pltpu.HBM((owners, 2, rows, wide), jnp.bfloat16),
        grid_spec=pltpu.PrefetchScalarGridSpec(
            num_scalar_prefetch=1,
            grid=(1,),
            in_specs=[pl.BlockSpec(memory_space=pl.ANY)] + [local] * (len(slabs) + 2),
            out_specs=pl.BlockSpec((owners, 2, rows, wide), lambda k, s: (0, 0, 0, 0)),
            scratch_shapes=[
                pltpu.VMEM((len(slabs), lines, depth), jnp.bfloat16),
                pltpu.VMEM((lines, wide), jnp.float32),
                pltpu.SemaphoreType.DMA((len(slabs),)),
            ],
        ),
        compiler_params=pltpu.CompilerParams(vmem_limit_bytes=26 << 20),
        cost_estimate=pl.CostEstimate(
            flops=2 * lines * depth * len(slabs) * wide,
            transcendentals=0,
            bytes_accessed=2 * lines * depth * len(slabs),
        ),
    )(places, in_hbm(signals), *slabs, partial, pack)


def attention_kernel(heads, fill_ref, cos_ref, sin_ref, q_ref, k_new_ref, v_new_ref, k_ref, v_ref, out_ref,
                     q_rot, k_rot, v_new, cached_scores, new_scores, blended):
    n_tp = q_ref.shape[1]
    block = ROW_BLOCK
    scale = HEAD ** (-0.5)
    width = 2 * heads
    first = pl.program_id(0) * block
    size = block * width

    def both(ref, t, step, start):
        lanes = slice(start, start + HEAD)
        return ref[0, t, step, :, lanes].astype(jnp.float32) + ref[1, t, step, :, lanes].astype(jnp.float32)

    def turned(values, step):
        turn = values * cos_ref[step] + pltpu.roll(values, HEAD // 2, 1) * sin_ref[step]
        return turn.astype(jnp.bfloat16).astype(jnp.float32)

    place = lax.broadcasted_iota(jnp.int32, (width, HEAD), 1)
    line = lax.broadcasted_iota(jnp.int32, (size, 2 * block), 0)
    column = lax.broadcasted_iota(jnp.int32, (size, 2 * block), 1)
    seen = ((column % block) == (line // width)) & (
        (column < block) | (line % width >= heads)
    )
    filled = [place < fill_ref[first + i] for i in range(block)]

    for t in range(n_tp):
        for step in range(2):
            for head in range(heads):
                at = pl.ds(t * size + (step * heads + head) * block, block)
                q_rot[at, :] = turned(both(q_ref, t, step, head * HEAD), step)
            at = pl.ds(step * block, block)
            k_rot[t, at, :] = turned(both(k_new_ref, t, step, 0), step)
            v_new[t, at, :] = both(v_new_ref, t, step, 0)
    for t in range(n_tp):
        lanes = slice(t * HEAD, (t + 1) * HEAD)
        queries = [
            q_rot[pl.ds(t * size + i, width, stride=block), :].astype(jnp.bfloat16) for i in range(block)
        ]
        for i in range(block):
            scores = lax.dot_general(
                queries[i], k_ref[i, :, lanes], NT, preferred_element_type=jnp.float32
            ) * scale
            cached_scores[t, pl.ds(i * width, width), :] = jnp.where(filled[i], scores, -1e30)
        scores = lax.dot_general(
            jnp.concatenate(queries, 0), k_rot[t].astype(jnp.bfloat16), NT,
            preferred_element_type=jnp.float32,
        ) * scale
        new_scores[t] = jnp.where(seen, scores, -1e30)
    for t in range(n_tp):
        lanes = slice(t * HEAD, (t + 1) * HEAD)
        cached, new = cached_scores[t], new_scores[t]
        top = jnp.maximum(jnp.max(cached, -1, keepdims=True), jnp.max(new, -1, keepdims=True))
        cached, new = jnp.exp(cached - top), jnp.exp(new - top)
        share = 1.0 / (jnp.sum(cached, -1, keepdims=True) + jnp.sum(new, -1, keepdims=True))
        cached, new = (cached * share).astype(jnp.bfloat16), (new * share).astype(jnp.bfloat16)
        from_new = jnp.dot(new, v_new[t].astype(jnp.bfloat16), preferred_element_type=jnp.float32)
        for i in range(block):
            part = slice(i * width, (i + 1) * width)
            mixed = jnp.dot(cached[part], v_ref[i, :, lanes], preferred_element_type=jnp.float32)
            blended[pl.ds(t * size + i, width, stride=block), :] = mixed + from_new[part]
    for t in range(n_tp):
        for step in range(2):
            for head in range(heads):
                at = pl.ds(t * size + (step * heads + head) * block, block)
                done = blended[at, :].astype(jnp.bfloat16)
                for pair in range(2):
                    out_ref[pair, t, step, :, head * HEAD:(head + 1) * HEAD] = done


def attend(fill, cosine, sine, queries, new, new_at, keys, values, heads):
    _, n_tp, _, rows, _ = queries.shape
    places = keys.shape[1]
    block = ROW_BLOCK
    width = 2 * heads * block
    table = pl.BlockSpec((2, block, HEAD), lambda r, f: (0, r, 0))
    cache = pl.BlockSpec((block, places, n_tp * HEAD), lambda r, f: (r, 0, 0))

    def routed(columns, at=0):
        return pl.BlockSpec((2, n_tp, 2, block, columns), lambda r, f: (0, 0, 0, r, at))

    return pl.pallas_call(
        functools.partial(attention_kernel, heads),
        out_shape=pltpu.HBM((2, n_tp, 2, rows, heads * HEAD), jnp.bfloat16),
        grid_spec=pltpu.PrefetchScalarGridSpec(
            num_scalar_prefetch=1,
            grid=(rows // block,),
            in_specs=[
                table, table, routed(heads * HEAD), routed(HEAD, new_at), routed(HEAD, new_at + 1),
                cache, cache,
            ],
            out_specs=routed(heads * HEAD),
            scratch_shapes=[
                pltpu.VMEM((n_tp * width, HEAD), jnp.float32),
                pltpu.VMEM((n_tp, 2 * block, HEAD), jnp.float32),
                pltpu.VMEM((n_tp, 2 * block, HEAD), jnp.float32),
                pltpu.VMEM((n_tp, width, HEAD), jnp.float32),
                pltpu.VMEM((n_tp, width, 2 * block), jnp.float32),
                pltpu.VMEM((n_tp * width, HEAD), jnp.float32),
            ],
        ),
        compiler_params=pltpu.CompilerParams(vmem_limit_bytes=18 << 20),
        cost_estimate=pl.CostEstimate(
            flops=8 * heads * rows * n_tp * places * HEAD,
            transcendentals=2 * heads * rows * n_tp * places,
            bytes_accessed=4 * rows * places * n_tp * HEAD,
        ),
    )(
        fill, cosine, sine, in_hbm(queries), in_hbm(new), in_hbm(new), in_hbm(keys), in_hbm(values)
    )


def unpack_kernel(owners, rows, pick_ref, back_ref, *refs):
    out_ref, gathered = refs[-2:]
    for owner in range(owners):
        gathered[pl.ds(owner * rows, rows), :] = back_ref[owner, 0].astype(jnp.float32)
    picked = jnp.dot(
        pick_ref[...], gathered[...].astype(jnp.bfloat16), preferred_element_type=jnp.float32
    )
    out_ref[0] = picked.astype(jnp.bfloat16)


def unpack(pick, back, at, columns, so_far):
    owners, _, rows, wide = back.shape
    share, slots = pick.shape
    before = [] if so_far is None else [so_far]
    return pl.pallas_call(
        functools.partial(unpack_kernel, owners, rows),
        out_shape=jax.ShapeDtypeStruct((2, share, columns), jnp.bfloat16),
        grid=(2,),
        in_specs=[
            pl.BlockSpec((share, slots), lambda s: (0, 0)),
            pl.BlockSpec((owners, 1, rows, wide), lambda s: (0, s, 0, 0)),
        ] + [pl.BlockSpec(memory_space=pl.ANY)] * len(before),
        out_specs=pl.BlockSpec((1, share, wide), lambda s: (s, 0, at)),
        scratch_shapes=[pltpu.VMEM((slots, wide), jnp.float32)],
        input_output_aliases={2: 0} if before else {},
        compiler_params=pltpu.CompilerParams(vmem_limit_bytes=8 << 20),
        cost_estimate=pl.CostEstimate(
            flops=4 * share * slots * wide, transcendentals=0, bytes_accessed=4 * slots * wide
        ),
    )(pick, back, *before)


def per_device(signals, matrix, offset, cached_keys, cached_values, fill, lines):
    n_pair, n_tp, n_grp = (int(lax.axis_size(a)) for a in ("pair", "tp", "grp"))
    pair, grp = (lax.axis_index(a) for a in ("pair", "grp"))
    share, features = signals.shape[1:]
    half, columns = matrix.shape
    rows = fill.shape[0]
    owners = n_pair * n_tp
    depth = half // n_grp

    def after(value, *earlier):
        return lax.optimization_barrier((value, *earlier))[0]

    flat = signals.reshape(2 * share, features)
    listed = lax.dynamic_slice_in_dim(lines, pair * share, share)
    slots = jnp.arange(owners * rows, dtype=jnp.int32)
    pack = (slots[:, None] == listed[None, :]).astype(jnp.bfloat16)
    pick = (listed[:, None] == slots[None, :]).astype(jnp.bfloat16)
    positions = fill[None, :] + jnp.arange(2, dtype=jnp.int32)[:, None]
    cosine, sine = rope_tables(positions)

    def exchange(blocks):
        return lax.all_to_all(blocks, ("pair", "tp"), split_axis=0, concat_axis=0, tiled=True)

    spans = [(a * HEAD, (b + 2 if b == SHARING else b) * HEAD) for a, b in CHUNKS]
    n_z = n_grp // 2
    up = [(2 * a + c, 2 * ((a + 1) % n_z) + c) for a in range(n_z) for c in range(2)]
    down = [(d, s) for s, d in up]
    twin = [(2 * a + c, 2 * a + 1 - c) for a in range(n_z) for c in range(2)]
    z, core = grp // 2, grp % 2
    turns = (0, n_z - 1, 1, 2)
    slab_of = [(z + turn) % n_z * 2 + core for turn in turns]
    places = (1 - pair) * n_grp + jnp.stack(
        slab_of + [(z + turn) % n_z * 2 + 1 - core for turn in turns]
    )
    places = places.astype(jnp.int32)

    def slab(at, span):
        return lax.dynamic_slice(matrix, (at * depth, span[0]), (depth, span[1] - span[0]))

    near = lax.dynamic_slice_in_dim(flat, pair * half, half, 1)
    partials = [
        jnp.dot(near, matrix[:, slice(*span)], preferred_element_type=jnp.float32)
        + offset[slice(*span)].astype(jnp.float32)
        for span in spans
    ]

    crossed = []
    for distance in (0, 3):
        for number, span in enumerate(spans):
            with jax.named_scope("over_pair_%d" % number):
                piece = after(slab(slab_of[distance], span), *crossed[-1:])
                crossed.append(lax.ppermute(piece, "pair", SWAP))
    crossed[0] = after(crossed[0], *partials)
    held = []
    for number in range(len(spans)):
        own, far = crossed[number], crossed[len(spans) + number]
        with jax.named_scope("from_neighbours_%d" % number):
            below = lax.ppermute(own, "grp", up)
            above = lax.ppermute(own, "grp", down)
        with jax.named_scope("from_twin_%d" % number):
            four = [own, below, above, far]
            held.append(four + [lax.ppermute(piece, "grp", twin) for piece in four])
    arrived = []
    for number, (span, slabs) in enumerate(zip(spans, held)):
        with jax.named_scope("project_%d" % number):
            packed = project(places, flat, slabs, partials[number], pack, owners)
        with jax.named_scope("route_%d" % number):
            arrived.append(exchange(packed).reshape(n_pair, n_tp, 2, rows, span[1] - span[0]))
    out = None
    for (first, last), queries in zip(CHUNKS, arrived):
        heads = last - first
        attended = attend(
            fill, cosine, sine, queries, arrived[0], SHARING - CHUNKS[0][0],
            cached_keys, cached_values, heads,
        )
        back = exchange(attended.reshape(owners, 2, rows, heads * HEAD))
        out = unpack(pick, back, first // heads, SHARING * HEAD, out)
    return out


def solution(mesh):
    in_specs = (
        P(None, ("grp", "pair"), None),
        P("pair", "tp"),
        P("tp"),
        P(("grp", "pair", "tp"), None, None),
        P(("grp", "pair", "tp"), None, None),
        P(("grp", "pair", "tp")),
        P("grp"),
    )
    out_specs = P(None, ("grp", "pair"), "tp")
    return jax.shard_map(
        per_device, mesh=mesh, in_specs=in_specs, out_specs=out_specs, check_vma=False
    )
```

```python
import functools

import jax
import jax.numpy as jnp
from jax import lax
from jax.experimental import pallas as pl
from jax.experimental.pallas import tpu as pltpu
from jax.sharding import PartitionSpec as P

HEAD = 128
SHARING = 8
ROPE_BASE = 1000000.0
SWAP = ((0, 1), (1, 0))
CHUNKS = ((0, 4), (4, 8))
ROW_BLOCK = 8
NT = (((1,), (1,)), ((), ()))


def in_hbm(value):
    return pltpu.with_memory_space_constraint(value, pltpu.HBM)


def rope_tables(positions):
    frequency = ROPE_BASE ** (-jnp.arange(0, HEAD, 2, dtype=jnp.float32) / HEAD)
    angles = positions.astype(jnp.float32)[..., None] * frequency
    cosine = jnp.cos(angles)
    sine = jnp.sin(angles)
    return jnp.concatenate([cosine, cosine], -1), jnp.concatenate([-sine, sine], -1)


def project_kernel(owners, rows, places_ref, x_ref, *refs):
    slabs = refs[:-7]
    partial_ref, pack_ref, out_ref, taken, met, total, arrived = refs[-7:]
    depth = slabs[0].shape[0]
    share = pack_ref.shape[1]
    copies = []
    for i, slab in enumerate(slabs):
        first = pl.multiple_of(places_ref[i] * depth, depth)
        copies.append((
            pltpu.make_async_copy(x_ref.at[:, pl.ds(first, depth)], taken.at[i], arrived.at[0, i]),
            pltpu.make_async_copy(slab, met.at[i], arrived.at[1, i]),
        ))
        for copy in copies[i]:
            copy.start()
    for i in range(len(slabs)):
        for copy in copies[i]:
            copy.wait()
        product = jnp.dot(taken[i], met[i], preferred_element_type=jnp.float32)
        if i == 0:
            total[...] = partial_ref[...] + product
        else:
            total[...] += product
    for step in range(2):
        rounded = total[pl.ds(step * share, share), :].astype(jnp.bfloat16)
        packed = jnp.dot(pack_ref[...], rounded, preferred_element_type=jnp.float32)
        for owner in range(owners):
            block = packed[owner * rows:(owner + 1) * rows]
            out_ref[owner, step] = block.astype(jnp.bfloat16)


def project(places, signals, slabs, partial, pack, owners):
    lines, _ = signals.shape
    depth, wide = slabs[0].shape
    slots, share = pack.shape
    rows = slots // owners
    count = len(slabs)
    return pl.pallas_call(
        functools.partial(project_kernel, owners, rows),
        out_shape=pltpu.HBM((owners, 2, rows, wide), jnp.bfloat16),
        grid_spec=pltpu.PrefetchScalarGridSpec(
            num_scalar_prefetch=1,
            grid=(1,),
            in_specs=[pl.BlockSpec(memory_space=pl.ANY)] * (count + 1) + [
                pl.BlockSpec((lines, wide), lambda k, s: (0, 0)),
                pl.BlockSpec((slots, share), lambda k, s: (0, 0)),
            ],
            out_specs=pl.BlockSpec((owners, 2, rows, wide), lambda k, s: (0, 0, 0, 0)),
            scratch_shapes=[
                pltpu.VMEM((count, lines, depth), jnp.bfloat16),
                pltpu.VMEM((count, depth, wide), jnp.bfloat16),
                pltpu.VMEM((lines, wide), jnp.float32),
                pltpu.SemaphoreType.DMA((2, count)),
            ],
        ),
        compiler_params=pltpu.CompilerParams(vmem_limit_bytes=26 << 20),
        cost_estimate=pl.CostEstimate(
            flops=2 * lines * depth * count * wide,
            transcendentals=0,
            bytes_accessed=2 * (lines + wide) * depth * count,
        ),
    )(places, in_hbm(signals), *(in_hbm(slab) for slab in slabs), in_hbm(partial), in_hbm(pack))


def attention_kernel(heads, fill_ref, cos_ref, sin_ref, q_ref, k_new_ref, v_new_ref, k_ref, v_ref, out_ref,
                     q_rot, k_rot, v_new, cached_scores, new_scores, blended):
    n_tp = q_ref.shape[1]
    block = ROW_BLOCK
    scale = HEAD ** (-0.5)
    width = 2 * heads
    first = pl.program_id(0) * block
    size = block * width

    def both(ref, t, step, start):
        lanes = slice(start, start + HEAD)
        return ref[0, t, step, :, lanes].astype(jnp.float32) + ref[1, t, step, :, lanes].astype(jnp.float32)

    def turned(values, step):
        turn = values * cos_ref[step] + pltpu.roll(values, HEAD // 2, 1) * sin_ref[step]
        return turn.astype(jnp.bfloat16).astype(jnp.float32)

    place = lax.broadcasted_iota(jnp.int32, (width, HEAD), 1)
    line = lax.broadcasted_iota(jnp.int32, (size, 2 * block), 0)
    column = lax.broadcasted_iota(jnp.int32, (size, 2 * block), 1)
    seen = ((column % block) == (line // width)) & (
        (column < block) | (line % width >= heads)
    )
    filled = [place < fill_ref[first + i] for i in range(block)]

    for t in range(n_tp):
        for step in range(2):
            for head in range(heads):
                at = pl.ds(t * size + (step * heads + head) * block, block)
                q_rot[at, :] = turned(both(q_ref, t, step, head * HEAD), step)
            at = pl.ds(step * block, block)
            k_rot[t, at, :] = turned(both(k_new_ref, t, step, 0), step)
            v_new[t, at, :] = both(v_new_ref, t, step, 0)
    for t in range(n_tp):
        lanes = slice(t * HEAD, (t + 1) * HEAD)
        queries = [
            q_rot[pl.ds(t * size + i, width, stride=block), :].astype(jnp.bfloat16) for i in range(block)
        ]
        for i in range(block):
            scores = lax.dot_general(
                queries[i], k_ref[i, :, lanes], NT, preferred_element_type=jnp.float32
            ) * scale
            cached_scores[t, pl.ds(i * width, width), :] = jnp.where(filled[i], scores, -1e30)
        scores = lax.dot_general(
            jnp.concatenate(queries, 0), k_rot[t].astype(jnp.bfloat16), NT,
            preferred_element_type=jnp.float32,
        ) * scale
        new_scores[t] = jnp.where(seen, scores, -1e30)
    for t in range(n_tp):
        lanes = slice(t * HEAD, (t + 1) * HEAD)
        cached, new = cached_scores[t], new_scores[t]
        top = jnp.maximum(jnp.max(cached, -1, keepdims=True), jnp.max(new, -1, keepdims=True))
        cached, new = jnp.exp(cached - top), jnp.exp(new - top)
        share = 1.0 / (jnp.sum(cached, -1, keepdims=True) + jnp.sum(new, -1, keepdims=True))
        cached, new = (cached * share).astype(jnp.bfloat16), (new * share).astype(jnp.bfloat16)
        from_new = jnp.dot(new, v_new[t].astype(jnp.bfloat16), preferred_element_type=jnp.float32)
        for i in range(block):
            part = slice(i * width, (i + 1) * width)
            mixed = jnp.dot(cached[part], v_ref[i, :, lanes], preferred_element_type=jnp.float32)
            blended[pl.ds(t * size + i, width, stride=block), :] = mixed + from_new[part]
    for t in range(n_tp):
        for step in range(2):
            for head in range(heads):
                at = pl.ds(t * size + (step * heads + head) * block, block)
                done = blended[at, :].astype(jnp.bfloat16)
                for pair in range(2):
                    out_ref[pair, t, step, :, head * HEAD:(head + 1) * HEAD] = done


def attend(fill, cosine, sine, queries, new, keys, values, heads):
    _, n_tp, _, rows, _ = queries.shape
    places = keys.shape[1]
    block = ROW_BLOCK
    width = 2 * heads * block
    table = pl.BlockSpec((2, block, HEAD), lambda r, f: (0, r, 0))
    cache = pl.BlockSpec((block, places, n_tp * HEAD), lambda r, f: (r, 0, 0))

    def routed(columns, at=0):
        return pl.BlockSpec((2, n_tp, 2, block, columns), lambda r, f: (0, 0, 0, r, at))

    return pl.pallas_call(
        functools.partial(attention_kernel, heads),
        out_shape=pltpu.HBM((2, n_tp, 2, rows, heads * HEAD), jnp.bfloat16),
        grid_spec=pltpu.PrefetchScalarGridSpec(
            num_scalar_prefetch=1,
            grid=(rows // block,),
            in_specs=[
                table, table, routed(heads * HEAD), routed(HEAD, 0), routed(HEAD, 1),
                cache, cache,
            ],
            out_specs=routed(heads * HEAD),
            scratch_shapes=[
                pltpu.VMEM((n_tp * width, HEAD), jnp.float32),
                pltpu.VMEM((n_tp, 2 * block, HEAD), jnp.float32),
                pltpu.VMEM((n_tp, 2 * block, HEAD), jnp.float32),
                pltpu.VMEM((n_tp, width, HEAD), jnp.float32),
                pltpu.VMEM((n_tp, width, 2 * block), jnp.float32),
                pltpu.VMEM((n_tp * width, HEAD), jnp.float32),
            ],
        ),
        compiler_params=pltpu.CompilerParams(vmem_limit_bytes=18 << 20),
        cost_estimate=pl.CostEstimate(
            flops=8 * heads * rows * n_tp * places * HEAD,
            transcendentals=2 * heads * rows * n_tp * places,
            bytes_accessed=4 * rows * places * n_tp * HEAD,
        ),
    )(
        fill, cosine, sine, in_hbm(queries), in_hbm(new), in_hbm(new), in_hbm(keys), in_hbm(values)
    )


def unpack_kernel(owners, rows, pick_ref, back_ref, *refs):
    out_ref, gathered = refs[-2:]
    for owner in range(owners):
        gathered[pl.ds(owner * rows, rows), :] = back_ref[owner, 0].astype(jnp.float32)
    picked = jnp.dot(
        pick_ref[...], gathered[...].astype(jnp.bfloat16), preferred_element_type=jnp.float32
    )
    out_ref[0] = picked.astype(jnp.bfloat16)


def unpack(pick, back, at, columns, so_far):
    owners, _, rows, wide = back.shape
    share, slots = pick.shape
    before = [] if so_far is None else [so_far]
    return pl.pallas_call(
        functools.partial(unpack_kernel, owners, rows),
        out_shape=jax.ShapeDtypeStruct((2, share, columns), jnp.bfloat16),
        grid=(2,),
        in_specs=[
            pl.BlockSpec((share, slots), lambda s: (0, 0)),
            pl.BlockSpec((owners, 1, rows, wide), lambda s: (0, s, 0, 0)),
        ] + [pl.BlockSpec(memory_space=pl.ANY)] * len(before),
        out_specs=pl.BlockSpec((1, share, wide), lambda s: (s, 0, at)),
        scratch_shapes=[pltpu.VMEM((slots, wide), jnp.float32)],
        input_output_aliases={2: 0} if before else {},
        compiler_params=pltpu.CompilerParams(vmem_limit_bytes=8 << 20),
        cost_estimate=pl.CostEstimate(
            flops=4 * share * slots * wide, transcendentals=0, bytes_accessed=4 * slots * wide
        ),
    )(pick, back, *before)


def per_device(signals, matrix, offset, cached_keys, cached_values, fill, lines):
    n_pair, n_tp, n_grp = (int(lax.axis_size(a)) for a in ("pair", "tp", "grp"))
    pair, grp = (lax.axis_index(a) for a in ("pair", "grp"))
    share, features = signals.shape[1:]
    half, columns = matrix.shape
    rows = fill.shape[0]
    owners = n_pair * n_tp
    depth = half // n_grp

    def after(value, *earlier):
        return lax.optimization_barrier((value, *earlier))[0]

    flat = signals.reshape(2 * share, features)
    listed = lax.dynamic_slice_in_dim(lines, pair * share, share)
    slots = jnp.arange(owners * rows, dtype=jnp.int32)
    pack = (slots[:, None] == listed[None, :]).astype(jnp.bfloat16)
    pick = (listed[:, None] == slots[None, :]).astype(jnp.bfloat16)
    positions = fill[None, :] + jnp.arange(2, dtype=jnp.int32)[:, None]
    cosine, sine = rope_tables(positions)

    def exchange(blocks):
        return lax.all_to_all(blocks, ("pair", "tp"), split_axis=0, concat_axis=0, tiled=True)

    spans = [(SHARING * HEAD, columns)] + [(a * HEAD, b * HEAD) for a, b in CHUNKS]
    n_z = n_grp // 2
    up = [(2 * a + c, 2 * ((a + 1) % n_z) + c) for a in range(n_z) for c in range(2)]
    down = [(d, s) for s, d in up]
    twin = [(2 * a + c, 2 * a + 1 - c) for a in range(n_z) for c in range(2)]
    z, core = grp // 2, grp % 2
    turns = (0, n_z - 1, 1, 2)
    places = (1 - pair) * n_grp + jnp.stack(
        [(z + turn) % n_z * 2 + core for turn in turns]
        + [(z + turn) % n_z * 2 + 1 - core for turn in turns]
    )
    places = places.astype(jnp.int32)

    near = lax.dynamic_slice_in_dim(flat, pair * half, half, 1)
    partials = [
        jnp.dot(near, matrix[:, slice(*span)], preferred_element_type=jnp.float32)
        + offset[slice(*span)].astype(jnp.float32)
        for span in spans
    ]

    crossed = []
    for number, (start, stop) in enumerate(spans):
        with jax.named_scope("over_pair_%d" % number):
            slab = lax.dynamic_slice(matrix, (grp * depth, start), (depth, stop - start))
            crossed.append(lax.ppermute(after(slab, *crossed[-1:]), "pair", SWAP))
    ring, ahead = [], []
    for number, slab in enumerate(crossed):
        slab = after(slab, partials[number], *ahead)
        with jax.named_scope("from_below_%d" % number):
            below = lax.ppermute(slab, "grp", up)
        with jax.named_scope("from_above_%d" % number):
            above = lax.ppermute(slab, "grp", down)
        with jax.named_scope("from_opposite_%d" % number):
            if number % 2:
                opposite = lax.ppermute(above, "grp", down)
            else:
                opposite = lax.ppermute(below, "grp", up)
        ahead = [below, above] if number else [below, above, opposite]
        ring.append([slab, below, above, opposite])
    partials[0] = after(partials[0], crossed[2], ring[1][3], ring[2][1])
    arrived = []
    for number, (span, four) in enumerate(zip(spans, ring)):
        with jax.named_scope("from_twin_%d" % number):
            slabs = four + [lax.ppermute(piece, "grp", twin) for piece in four]
        with jax.named_scope("project_%d" % number):
            packed = project(places, flat, slabs, partials[number], pack, owners)
        with jax.named_scope("route_%d" % number):
            arrived.append(exchange(packed).reshape(n_pair, n_tp, 2, rows, span[1] - span[0]))
    out = None
    for (first, last), queries in zip(CHUNKS, arrived[1:]):
        heads = last - first
        attended = attend(
            fill, cosine, sine, queries, arrived[0], cached_keys, cached_values, heads
        )
        back = exchange(attended.reshape(owners, 2, rows, heads * HEAD))
        out = unpack(pick, back, first // heads, SHARING * HEAD, out)
    return out


def solution(mesh):
    in_specs = (
        P(None, ("grp", "pair"), None),
        P("pair", "tp"),
        P("tp"),
        P(("grp", "pair", "tp"), None, None),
        P(("grp", "pair", "tp"), None, None),
        P(("grp", "pair", "tp")),
        P("grp"),
    )
    out_specs = P(None, ("grp", "pair"), "tp")
    return jax.shard_map(
        per_device, mesh=mesh, in_specs=in_specs, out_specs=out_specs, check_vma=False
    )
```

```python
import functools

import jax
import jax.numpy as jnp
from jax import lax
from jax.experimental import pallas as pl
from jax.experimental.pallas import tpu as pltpu
from jax.sharding import PartitionSpec as P

HEAD = 128
SHARING = 8
ROPE_BASE = 1000000.0
SWAP = ((0, 1), (1, 0))
CHUNKS = ((0, 4), (4, 8))
ROW_BLOCK = 8
NT = (((1,), (1,)), ((), ()))


def in_hbm(value):
    return pltpu.with_memory_space_constraint(value, pltpu.HBM)


def rope_tables(positions):
    frequency = ROPE_BASE ** (-jnp.arange(0, HEAD, 2, dtype=jnp.float32) / HEAD)
    angles = positions.astype(jnp.float32)[..., None] * frequency
    cosine = jnp.cos(angles)
    sine = jnp.sin(angles)
    return jnp.concatenate([cosine, cosine], -1), jnp.concatenate([-sine, sine], -1)


def project_kernel(parts, owners, rows, places_ref, x_ref, *refs):
    slabs, refs = refs[:-(parts + 6)], refs[-(parts + 6):]
    partials = refs[:parts]
    pack_ref, out_ref, taken, met, total, arrived = refs[parts:]
    count = taken.shape[0]
    depth = met.shape[1]
    share = pack_ref.shape[1]
    spans, at = [], 0
    for part in partials:
        spans.append((at, part.shape[1]))
        at += part.shape[1]
    copies = []
    for i in range(count):
        first = pl.multiple_of(places_ref[i] * depth, depth)
        copies.append([
            pltpu.make_async_copy(x_ref.at[:, pl.ds(first, depth)], taken.at[i], arrived.at[0, i])
        ])
        for part, (start, wide) in enumerate(spans):
            copies[i].append(
                pltpu.make_async_copy(
                    slabs[part * count + i], met.at[i, :, pl.ds(start, wide)],
                    arrived.at[part + 1, i],
                )
            )
        for copy in copies[i]:
            copy.start()
    for i in range(count):
        for copy in copies[i]:
            copy.wait()
        product = jnp.dot(taken[i], met[i], preferred_element_type=jnp.float32)
        if i == 0:
            for part, (start, wide) in zip(partials, spans):
                columns = slice(start, start + wide)
                total[:, columns] = part[...] + product[:, columns]
        else:
            total[...] += product
    for step in range(2):
        rounded = total[pl.ds(step * share, share), :].astype(jnp.bfloat16)
        packed = jnp.dot(pack_ref[...], rounded, preferred_element_type=jnp.float32)
        for owner in range(owners):
            block = packed[owner * rows:(owner + 1) * rows]
            out_ref[owner, step] = block.astype(jnp.bfloat16)


def project(places, signals, slabs, partials, pack, owners):
    lines, _ = signals.shape
    count, parts = len(slabs[0]), len(slabs)
    depth = slabs[0][0].shape[0]
    wide = sum(partial.shape[1] for partial in partials)
    slots, share = pack.shape
    rows = slots // owners
    return pl.pallas_call(
        functools.partial(project_kernel, parts, owners, rows),
        out_shape=pltpu.HBM((owners, 2, rows, wide), jnp.bfloat16),
        grid_spec=pltpu.PrefetchScalarGridSpec(
            num_scalar_prefetch=1,
            grid=(1,),
            in_specs=[pl.BlockSpec(memory_space=pl.ANY)] * (1 + parts * count) + [
                pl.BlockSpec(partial.shape, lambda k, s: (0, 0)) for partial in partials
            ] + [pl.BlockSpec((slots, share), lambda k, s: (0, 0))],
            out_specs=pl.BlockSpec((owners, 2, rows, wide), lambda k, s: (0, 0, 0, 0)),
            scratch_shapes=[
                pltpu.VMEM((count, lines, depth), jnp.bfloat16),
                pltpu.VMEM((count, depth, wide), jnp.bfloat16),
                pltpu.VMEM((lines, wide), jnp.float32),
                pltpu.SemaphoreType.DMA((parts + 1, count)),
            ],
        ),
        compiler_params=pltpu.CompilerParams(vmem_limit_bytes=30 << 20),
        cost_estimate=pl.CostEstimate(
            flops=2 * lines * depth * count * wide,
            transcendentals=0,
            bytes_accessed=2 * (lines + wide) * depth * count,
        ),
    )(
        places, in_hbm(signals), *(in_hbm(slab) for part in slabs for slab in part),
        *(in_hbm(partial) for partial in partials), in_hbm(pack),
    )


def attention_kernel(heads, fill_ref, cos_ref, sin_ref, q_ref, k_new_ref, v_new_ref, k_ref, v_ref, out_ref,
                     q_rot, k_rot, v_new, cached_scores, new_scores, blended):
    n_tp = q_ref.shape[1]
    block = ROW_BLOCK
    scale = HEAD ** (-0.5)
    width = 2 * heads
    first = pl.program_id(0) * block
    size = block * width

    def both(ref, t, step, start):
        lanes = slice(start, start + HEAD)
        return ref[0, t, step, :, lanes].astype(jnp.float32) + ref[1, t, step, :, lanes].astype(jnp.float32)

    def turned(values, step):
        turn = values * cos_ref[step] + pltpu.roll(values, HEAD // 2, 1) * sin_ref[step]
        return turn.astype(jnp.bfloat16).astype(jnp.float32)

    place = lax.broadcasted_iota(jnp.int32, (width, HEAD), 1)
    line = lax.broadcasted_iota(jnp.int32, (size, 2 * block), 0)
    column = lax.broadcasted_iota(jnp.int32, (size, 2 * block), 1)
    seen = ((column % block) == (line // width)) & (
        (column < block) | (line % width >= heads)
    )
    filled = [place < fill_ref[first + i] for i in range(block)]

    for t in range(n_tp):
        for step in range(2):
            for head in range(heads):
                at = pl.ds(t * size + (step * heads + head) * block, block)
                q_rot[at, :] = turned(both(q_ref, t, step, head * HEAD), step)
            at = pl.ds(step * block, block)
            k_rot[t, at, :] = turned(both(k_new_ref, t, step, 0), step)
            v_new[t, at, :] = both(v_new_ref, t, step, 0)
    for t in range(n_tp):
        lanes = slice(t * HEAD, (t + 1) * HEAD)
        queries = [
            q_rot[pl.ds(t * size + i, width, stride=block), :].astype(jnp.bfloat16) for i in range(block)
        ]
        for i in range(block):
            scores = lax.dot_general(
                queries[i], k_ref[i, :, lanes], NT, preferred_element_type=jnp.float32
            ) * scale
            cached_scores[t, pl.ds(i * width, width), :] = jnp.where(filled[i], scores, -1e30)
        scores = lax.dot_general(
            jnp.concatenate(queries, 0), k_rot[t].astype(jnp.bfloat16), NT,
            preferred_element_type=jnp.float32,
        ) * scale
        new_scores[t] = jnp.where(seen, scores, -1e30)
    for t in range(n_tp):
        lanes = slice(t * HEAD, (t + 1) * HEAD)
        cached, new = cached_scores[t], new_scores[t]
        top = jnp.maximum(jnp.max(cached, -1, keepdims=True), jnp.max(new, -1, keepdims=True))
        cached, new = jnp.exp(cached - top), jnp.exp(new - top)
        share = 1.0 / (jnp.sum(cached, -1, keepdims=True) + jnp.sum(new, -1, keepdims=True))
        cached, new = (cached * share).astype(jnp.bfloat16), (new * share).astype(jnp.bfloat16)
        from_new = jnp.dot(new, v_new[t].astype(jnp.bfloat16), preferred_element_type=jnp.float32)
        for i in range(block):
            part = slice(i * width, (i + 1) * width)
            mixed = jnp.dot(cached[part], v_ref[i, :, lanes], preferred_element_type=jnp.float32)
            blended[pl.ds(t * size + i, width, stride=block), :] = mixed + from_new[part]
    for t in range(n_tp):
        for step in range(2):
            for head in range(heads):
                at = pl.ds(t * size + (step * heads + head) * block, block)
                done = blended[at, :].astype(jnp.bfloat16)
                for pair in range(2):
                    out_ref[pair, t, step, :, head * HEAD:(head + 1) * HEAD] = done


def attend(fill, cosine, sine, queries, new, new_at, keys, values, heads):
    _, n_tp, _, rows, _ = queries.shape
    places = keys.shape[1]
    block = ROW_BLOCK
    width = 2 * heads * block
    table = pl.BlockSpec((2, block, HEAD), lambda r, f: (0, r, 0))
    cache = pl.BlockSpec((block, places, n_tp * HEAD), lambda r, f: (r, 0, 0))

    def routed(columns, at=0):
        return pl.BlockSpec((2, n_tp, 2, block, columns), lambda r, f: (0, 0, 0, r, at))

    return pl.pallas_call(
        functools.partial(attention_kernel, heads),
        out_shape=pltpu.HBM((2, n_tp, 2, rows, heads * HEAD), jnp.bfloat16),
        grid_spec=pltpu.PrefetchScalarGridSpec(
            num_scalar_prefetch=1,
            grid=(rows // block,),
            in_specs=[
                table, table, routed(heads * HEAD), routed(HEAD, new_at), routed(HEAD, new_at + 1),
                cache, cache,
            ],
            out_specs=routed(heads * HEAD),
            scratch_shapes=[
                pltpu.VMEM((n_tp * width, HEAD), jnp.float32),
                pltpu.VMEM((n_tp, 2 * block, HEAD), jnp.float32),
                pltpu.VMEM((n_tp, 2 * block, HEAD), jnp.float32),
                pltpu.VMEM((n_tp, width, HEAD), jnp.float32),
                pltpu.VMEM((n_tp, width, 2 * block), jnp.float32),
                pltpu.VMEM((n_tp * width, HEAD), jnp.float32),
            ],
        ),
        compiler_params=pltpu.CompilerParams(vmem_limit_bytes=18 << 20),
        cost_estimate=pl.CostEstimate(
            flops=8 * heads * rows * n_tp * places * HEAD,
            transcendentals=2 * heads * rows * n_tp * places,
            bytes_accessed=4 * rows * places * n_tp * HEAD,
        ),
    )(
        fill, cosine, sine, in_hbm(queries), in_hbm(new), in_hbm(new), in_hbm(keys), in_hbm(values)
    )


def unpack_kernel(owners, rows, at, pick_ref, back_ref, *refs):
    out_ref, gathered, picked, written = refs[-4:]
    step = pl.program_id(0)
    for owner in range(owners):
        gathered[pl.ds(owner * rows, rows), :] = back_ref[owner, 0].astype(jnp.float32)
    picked[step] = jnp.dot(
        pick_ref[...], gathered[...].astype(jnp.bfloat16), preferred_element_type=jnp.float32
    ).astype(jnp.bfloat16)
    columns = pl.ds(at, picked.shape[2])
    copies = [
        pltpu.make_async_copy(picked.at[i], out_ref.at[i, :, columns], written.at[i])
        for i in range(2)
    ]

    @pl.when(step == 0)
    def _():
        copies[0].start()

    @pl.when(step == 1)
    def _():
        copies[1].start()
        copies[0].wait()
        copies[1].wait()


def unpack(pick, back, at, columns, so_far):
    owners, _, rows, wide = back.shape
    share, slots = pick.shape
    before = [] if so_far is None else [so_far]
    return pl.pallas_call(
        functools.partial(unpack_kernel, owners, rows, at),
        out_shape=jax.ShapeDtypeStruct((2, share, columns), jnp.bfloat16),
        grid=(2,),
        in_specs=[
            pl.BlockSpec((share, slots), lambda s: (0, 0)),
            pl.BlockSpec((owners, 1, rows, wide), lambda s: (0, s, 0, 0)),
        ] + [pl.BlockSpec(memory_space=pl.ANY)] * len(before),
        out_specs=pl.BlockSpec(memory_space=pl.ANY),
        scratch_shapes=[
            pltpu.VMEM((slots, wide), jnp.float32),
            pltpu.VMEM((2, share, wide), jnp.bfloat16),
            pltpu.SemaphoreType.DMA((2,)),
        ],
        input_output_aliases={2: 0} if before else {},
        compiler_params=pltpu.CompilerParams(vmem_limit_bytes=12 << 20),
        cost_estimate=pl.CostEstimate(
            flops=4 * share * slots * wide, transcendentals=0, bytes_accessed=4 * slots * wide
        ),
    )(pick, back, *before)


def per_device(signals, matrix, offset, cached_keys, cached_values, fill, lines):
    n_pair, n_tp, n_grp = (int(lax.axis_size(a)) for a in ("pair", "tp", "grp"))
    pair, grp = (lax.axis_index(a) for a in ("pair", "grp"))
    share, features = signals.shape[1:]
    half, columns = matrix.shape
    rows = fill.shape[0]
    owners = n_pair * n_tp
    depth = half // n_grp

    def after(value, *earlier):
        return lax.optimization_barrier((value, *earlier))[0]

    flat = signals.reshape(2 * share, features)
    listed = lax.dynamic_slice_in_dim(lines, pair * share, share)
    slots = jnp.arange(owners * rows, dtype=jnp.int32)
    pack = (slots[:, None] == listed[None, :]).astype(jnp.bfloat16)
    pick = (listed[:, None] == slots[None, :]).astype(jnp.bfloat16)
    positions = fill[None, :] + jnp.arange(2, dtype=jnp.int32)[:, None]
    cosine, sine = rope_tables(positions)

    def exchange(blocks):
        return lax.all_to_all(blocks, ("pair", "tp"), split_axis=0, concat_axis=0, tiled=True)

    spans = [(a * HEAD, b * HEAD) for a, b in CHUNKS]
    spans.insert(0, (SHARING * HEAD, columns))
    n_z = n_grp // 2
    up = [(2 * a + c, 2 * ((a + 1) % n_z) + c) for a in range(n_z) for c in range(2)]
    down = [(d, s) for s, d in up]
    twin = [(2 * a + c, 2 * a + 1 - c) for a in range(n_z) for c in range(2)]
    z, core = grp // 2, grp % 2
    held_of = [(z + turn) % n_z * 2 for turn in (0, n_z - 1, 1, 2)]
    places = (1 - pair) * n_grp + jnp.stack(
        [first + core for first in held_of] + [first + 1 - core for first in held_of]
    )
    places = places.astype(jnp.int32)

    near = lax.dynamic_slice_in_dim(flat, pair * half, half, 1)
    partials = [
        jnp.dot(near, matrix[:, slice(*span)], preferred_element_type=jnp.float32)
        + offset[slice(*span)].astype(jnp.float32)
        for span in spans
    ]

    crossed = []
    for number, (start, stop) in enumerate(spans):
        with jax.named_scope("over_pair_%d" % number):
            slab = lax.dynamic_slice(matrix, ((held_of[0] + core) * depth, start), (depth, stop - start))
            crossed.append(lax.ppermute(after(slab, *crossed[1:]), "pair", SWAP))
    ring, ahead = [], []
    for number, slab in enumerate(crossed):
        slab = after(slab, partials[number], *ahead)
        with jax.named_scope("from_below_%d" % number):
            below = lax.ppermute(slab, "grp", up)
        with jax.named_scope("from_above_%d" % number):
            above = lax.ppermute(slab, "grp", down)
        with jax.named_scope("from_opposite_%d" % number):
            if number % 2:
                opposite = lax.ppermute(above, "grp", down)
            else:
                opposite = lax.ppermute(below, "grp", up)
        ahead = [below, above] if number else [below, above, opposite]
        ring.append([slab, below, above, opposite])
    partials[0] = after(partials[0], crossed[2], ring[2][1])
    arrived = []
    for group in ((1, 0), (2,)):
        slabs = []
        for number in group:
            with jax.named_scope("from_twin_%d" % number):
                slabs.append(ring[number] + [lax.ppermute(piece, "grp", twin) for piece in ring[number]])
        with jax.named_scope("project_%d" % group[0]):
            packed = project(places, flat, slabs, [partials[number] for number in group], pack, owners)
        with jax.named_scope("route_%d" % group[0]):
            arrived.append(exchange(packed).reshape(n_pair, n_tp, 2, rows, packed.shape[-1]))
    out = None
    for (first, last), queries in zip(CHUNKS, arrived):
        heads = last - first
        attended = attend(
            fill, cosine, sine, queries, arrived[0], CHUNKS[0][1] - CHUNKS[0][0],
            cached_keys, cached_values, heads,
        )
        back = exchange(attended.reshape(owners, 2, rows, heads * HEAD))
        out = unpack(pick, back, first * HEAD, SHARING * HEAD, out)
    return out


def solution(mesh):
    in_specs = (
        P(None, ("grp", "pair"), None),
        P("pair", "tp"),
        P("tp"),
        P(("grp", "pair", "tp"), None, None),
        P(("grp", "pair", "tp"), None, None),
        P(("grp", "pair", "tp")),
        P("grp"),
    )
    out_specs = P(None, ("grp", "pair"), "tp")
    return jax.shard_map(
        per_device, mesh=mesh, in_specs=in_specs, out_specs=out_specs, check_vma=False
    )
```

```python
import functools

import jax
import jax.numpy as jnp
from jax import lax
from jax.experimental import pallas as pl
from jax.experimental.pallas import tpu as pltpu
from jax.sharding import PartitionSpec as P

HEAD = 128
SHARING = 8
ROPE_BASE = 1000000.0
SWAP = ((0, 1), (1, 0))
CHUNKS = ((0, 4), (4, 8))
ROW_BLOCK = 8
NT = (((1,), (1,)), ((), ()))


def in_hbm(value):
    return pltpu.with_memory_space_constraint(value, pltpu.HBM)


def rope_tables(positions):
    frequency = ROPE_BASE ** (-jnp.arange(0, HEAD, 2, dtype=jnp.float32) / HEAD)
    angles = positions.astype(jnp.float32)[..., None] * frequency
    cosine = jnp.cos(angles)
    sine = jnp.sin(angles)
    return jnp.concatenate([cosine, cosine], -1), jnp.concatenate([-sine, sine], -1)


def project_kernel(owners, rows, places_ref, x_ref, *refs):
    slabs = refs[:-7]
    partial_ref, pack_ref, out_ref, taken, met, total, arrived = refs[-7:]
    depth = slabs[0].shape[0]
    share = pack_ref.shape[1]
    copies = []
    for i, slab in enumerate(slabs):
        first = pl.multiple_of(places_ref[i] * depth, depth)
        copies.append((
            pltpu.make_async_copy(x_ref.at[:, pl.ds(first, depth)], taken.at[i], arrived.at[0, i]),
            pltpu.make_async_copy(slab, met.at[i], arrived.at[1, i]),
        ))
        for copy in copies[i]:
            copy.start()
    for i in range(len(slabs)):
        for copy in copies[i]:
            copy.wait()
        product = jnp.dot(taken[i], met[i], preferred_element_type=jnp.float32)
        if i == 0:
            total[...] = partial_ref[...] + product
        else:
            total[...] += product
    for step in range(2):
        rounded = total[pl.ds(step * share, share), :].astype(jnp.bfloat16)
        packed = jnp.dot(pack_ref[...], rounded, preferred_element_type=jnp.float32)
        for owner in range(owners):
            block = packed[owner * rows:(owner + 1) * rows]
            out_ref[owner, step] = block.astype(jnp.bfloat16)


def project(places, signals, slabs, partial, pack, owners):
    lines, _ = signals.shape
    depth, wide = slabs[0].shape
    slots, share = pack.shape
    rows = slots // owners
    count = len(slabs)
    return pl.pallas_call(
        functools.partial(project_kernel, owners, rows),
        out_shape=pltpu.HBM((owners, 2, rows, wide), jnp.bfloat16),
        grid_spec=pltpu.PrefetchScalarGridSpec(
            num_scalar_prefetch=1,
            grid=(1,),
            in_specs=[pl.BlockSpec(memory_space=pl.ANY)] * (count + 1) + [
                pl.BlockSpec((lines, wide), lambda k, s: (0, 0)),
                pl.BlockSpec((slots, share), lambda k, s: (0, 0)),
            ],
            out_specs=pl.BlockSpec((owners, 2, rows, wide), lambda k, s: (0, 0, 0, 0)),
            scratch_shapes=[
                pltpu.VMEM((count, lines, depth), jnp.bfloat16),
                pltpu.VMEM((count, depth, wide), jnp.bfloat16),
                pltpu.VMEM((lines, wide), jnp.float32),
                pltpu.SemaphoreType.DMA((2, count)),
            ],
        ),
        compiler_params=pltpu.CompilerParams(vmem_limit_bytes=26 << 20),
        cost_estimate=pl.CostEstimate(
            flops=2 * lines * depth * count * wide,
            transcendentals=0,
            bytes_accessed=2 * (lines + wide) * depth * count,
        ),
    )(places, in_hbm(signals), *(in_hbm(slab) for slab in slabs), in_hbm(partial), in_hbm(pack))


def attention_kernel(heads, fill_ref, cos_ref, sin_ref, q_ref, k_new_ref, v_new_ref, k_ref, v_ref, out_ref,
                     q_rot, k_rot, v_new, cached_scores, new_scores, blended):
    n_tp = q_ref.shape[1]
    block = ROW_BLOCK
    scale = HEAD ** (-0.5)
    width = 2 * heads
    first = pl.program_id(0) * block
    size = block * width

    def both(ref, t, step, start):
        lanes = slice(start, start + HEAD)
        return ref[0, t, step, :, lanes].astype(jnp.float32) + ref[1, t, step, :, lanes].astype(jnp.float32)

    def turned(values, step):
        turn = values * cos_ref[step] + pltpu.roll(values, HEAD // 2, 1) * sin_ref[step]
        return turn.astype(jnp.bfloat16).astype(jnp.float32)

    place = lax.broadcasted_iota(jnp.int32, (width, HEAD), 1)
    line = lax.broadcasted_iota(jnp.int32, (size, 2 * block), 0)
    column = lax.broadcasted_iota(jnp.int32, (size, 2 * block), 1)
    seen = ((column % block) == (line // width)) & (
        (column < block) | (line % width >= heads)
    )
    filled = [place < fill_ref[first + i] for i in range(block)]

    for t in range(n_tp):
        for step in range(2):
            for head in range(heads):
                at = pl.ds(t * size + (step * heads + head) * block, block)
                q_rot[at, :] = turned(both(q_ref, t, step, head * HEAD), step)
            at = pl.ds(step * block, block)
            k_rot[t, at, :] = turned(both(k_new_ref, t, step, 0), step)
            v_new[t, at, :] = both(v_new_ref, t, step, 0)
    for t in range(n_tp):
        lanes = slice(t * HEAD, (t + 1) * HEAD)
        queries = [
            q_rot[pl.ds(t * size + i, width, stride=block), :].astype(jnp.bfloat16) for i in range(block)
        ]
        for i in range(block):
            scores = lax.dot_general(
                queries[i], k_ref[i, :, lanes], NT, preferred_element_type=jnp.float32
            ) * scale
            cached_scores[t, pl.ds(i * width, width), :] = jnp.where(filled[i], scores, -1e30)
        scores = lax.dot_general(
            jnp.concatenate(queries, 0), k_rot[t].astype(jnp.bfloat16), NT,
            preferred_element_type=jnp.float32,
        ) * scale
        new_scores[t] = jnp.where(seen, scores, -1e30)
    for t in range(n_tp):
        lanes = slice(t * HEAD, (t + 1) * HEAD)
        cached, new = cached_scores[t], new_scores[t]
        top = jnp.maximum(jnp.max(cached, -1, keepdims=True), jnp.max(new, -1, keepdims=True))
        cached, new = jnp.exp(cached - top), jnp.exp(new - top)
        share = 1.0 / (jnp.sum(cached, -1, keepdims=True) + jnp.sum(new, -1, keepdims=True))
        cached, new = (cached * share).astype(jnp.bfloat16), (new * share).astype(jnp.bfloat16)
        from_new = jnp.dot(new, v_new[t].astype(jnp.bfloat16), preferred_element_type=jnp.float32)
        for i in range(block):
            part = slice(i * width, (i + 1) * width)
            mixed = jnp.dot(cached[part], v_ref[i, :, lanes], preferred_element_type=jnp.float32)
            blended[pl.ds(t * size + i, width, stride=block), :] = mixed + from_new[part]
    for t in range(n_tp):
        for step in range(2):
            for head in range(heads):
                at = pl.ds(t * size + (step * heads + head) * block, block)
                done = blended[at, :].astype(jnp.bfloat16)
                for pair in range(2):
                    out_ref[pair, t, step, :, head * HEAD:(head + 1) * HEAD] = done


def attend(fill, cosine, sine, queries, new, keys, values, heads):
    _, n_tp, _, rows, _ = queries.shape
    places = keys.shape[1]
    block = ROW_BLOCK
    width = 2 * heads * block
    table = pl.BlockSpec((2, block, HEAD), lambda r, f: (0, r, 0))
    cache = pl.BlockSpec((block, places, n_tp * HEAD), lambda r, f: (r, 0, 0))

    def routed(columns, at=0):
        return pl.BlockSpec((2, n_tp, 2, block, columns), lambda r, f: (0, 0, 0, r, at))

    return pl.pallas_call(
        functools.partial(attention_kernel, heads),
        out_shape=pltpu.HBM((2, n_tp, 2, rows, heads * HEAD), jnp.bfloat16),
        grid_spec=pltpu.PrefetchScalarGridSpec(
            num_scalar_prefetch=1,
            grid=(rows // block,),
            in_specs=[
                table, table, routed(heads * HEAD), routed(HEAD, 0), routed(HEAD, 1),
                cache, cache,
            ],
            out_specs=routed(heads * HEAD),
            scratch_shapes=[
                pltpu.VMEM((n_tp * width, HEAD), jnp.float32),
                pltpu.VMEM((n_tp, 2 * block, HEAD), jnp.float32),
                pltpu.VMEM((n_tp, 2 * block, HEAD), jnp.float32),
                pltpu.VMEM((n_tp, width, HEAD), jnp.float32),
                pltpu.VMEM((n_tp, width, 2 * block), jnp.float32),
                pltpu.VMEM((n_tp * width, HEAD), jnp.float32),
            ],
        ),
        compiler_params=pltpu.CompilerParams(vmem_limit_bytes=18 << 20),
        cost_estimate=pl.CostEstimate(
            flops=8 * heads * rows * n_tp * places * HEAD,
            transcendentals=2 * heads * rows * n_tp * places,
            bytes_accessed=4 * rows * places * n_tp * HEAD,
        ),
    )(
        fill, cosine, sine, in_hbm(queries), in_hbm(new), in_hbm(new), in_hbm(keys), in_hbm(values)
    )


def unpack_kernel(owners, rows, pick_ref, back_ref, *refs):
    out_ref, gathered = refs[-2:]
    for owner in range(owners):
        gathered[pl.ds(owner * rows, rows), :] = back_ref[owner, 0].astype(jnp.float32)
    picked = jnp.dot(
        pick_ref[...], gathered[...].astype(jnp.bfloat16), preferred_element_type=jnp.float32
    )
    out_ref[0] = picked.astype(jnp.bfloat16)


def unpack(pick, back, at, columns, so_far):
    owners, _, rows, wide = back.shape
    share, slots = pick.shape
    before = [] if so_far is None else [so_far]
    return pl.pallas_call(
        functools.partial(unpack_kernel, owners, rows),
        out_shape=jax.ShapeDtypeStruct((2, share, columns), jnp.bfloat16),
        grid=(2,),
        in_specs=[
            pl.BlockSpec((share, slots), lambda s: (0, 0)),
            pl.BlockSpec((owners, 1, rows, wide), lambda s: (0, s, 0, 0)),
        ] + [pl.BlockSpec(memory_space=pl.ANY)] * len(before),
        out_specs=pl.BlockSpec((1, share, wide), lambda s: (s, 0, at)),
        scratch_shapes=[pltpu.VMEM((slots, wide), jnp.float32)],
        input_output_aliases={2: 0} if before else {},
        compiler_params=pltpu.CompilerParams(vmem_limit_bytes=8 << 20),
        cost_estimate=pl.CostEstimate(
            flops=4 * share * slots * wide, transcendentals=0, bytes_accessed=4 * slots * wide
        ),
    )(pick, back, *before)


def per_device(signals, matrix, offset, cached_keys, cached_values, fill, lines):
    n_pair, n_tp, n_grp = (int(lax.axis_size(a)) for a in ("pair", "tp", "grp"))
    pair, grp = (lax.axis_index(a) for a in ("pair", "grp"))
    share, features = signals.shape[1:]
    half, columns = matrix.shape
    rows = fill.shape[0]
    owners = n_pair * n_tp
    depth = half // n_grp

    def after(value, *earlier):
        return lax.optimization_barrier((value, *earlier))[0]

    flat = signals.reshape(2 * share, features)
    listed = lax.dynamic_slice_in_dim(lines, pair * share, share)
    slots = jnp.arange(owners * rows, dtype=jnp.int32)
    pack = (slots[:, None] == listed[None, :]).astype(jnp.bfloat16)
    pick = (listed[:, None] == slots[None, :]).astype(jnp.bfloat16)
    positions = fill[None, :] + jnp.arange(2, dtype=jnp.int32)[:, None]
    cosine, sine = rope_tables(positions)

    def exchange(blocks):
        return lax.all_to_all(blocks, ("pair", "tp"), split_axis=0, concat_axis=0, tiled=True)

    spans = [(SHARING * HEAD, columns)] + [(a * HEAD, b * HEAD) for a, b in CHUNKS]
    n_z = n_grp // 2
    up = [(2 * a + c, 2 * ((a + 1) % n_z) + c) for a in range(n_z) for c in range(2)]
    down = [(d, s) for s, d in up]
    twin = [(2 * a + c, 2 * a + 1 - c) for a in range(n_z) for c in range(2)]
    z, core = grp // 2, grp % 2
    turns = (0, n_z - 1, 1, 2)
    places = (1 - pair) * n_grp + jnp.stack(
        [(z + turn) % n_z * 2 + core for turn in turns]
        + [(z + turn) % n_z * 2 + 1 - core for turn in turns]
    )
    places = places.astype(jnp.int32)

    near = lax.dynamic_slice_in_dim(flat, pair * half, half, 1)
    partials = [
        jnp.dot(near, matrix[:, slice(*span)], preferred_element_type=jnp.float32)
        + offset[slice(*span)].astype(jnp.float32)
        for span in spans
    ]

    crossed = []
    for number, (start, stop) in enumerate(spans):
        with jax.named_scope("over_pair_%d" % number):
            slab = lax.dynamic_slice(matrix, (grp * depth, start), (depth, stop - start))
            crossed.append(lax.ppermute(after(slab, *crossed[-1:]), "pair", SWAP))
    def neighbours(number, slab):
        with jax.named_scope("from_below_%d" % number):
            below = lax.ppermute(slab, "grp", up)
        with jax.named_scope("from_above_%d" % number):
            return below, lax.ppermute(slab, "grp", down)

    def further(number, piece, way):
        with jax.named_scope("from_opposite_%d" % number):
            return lax.ppermute(piece, "grp", way)

    arrived = []

    def finish(number, four):
        with jax.named_scope("from_twin_%d" % number):
            slabs = four + [lax.ppermute(piece, "grp", twin) for piece in four]
        with jax.named_scope("project_%d" % number):
            packed = project(places, flat, slabs, partials[number], pack, owners)
        with jax.named_scope("route_%d" % number):
            start, stop = spans[number]
            arrived.append(exchange(packed).reshape(n_pair, n_tp, 2, rows, stop - start))
        return packed

    slab0 = after(crossed[0], partials[0])
    below0, above0 = neighbours(0, slab0)
    opposite0 = further(0, below0, up)
    slab1 = after(crossed[1], partials[1], below0, above0, opposite0)
    below1, above1 = neighbours(1, slab1)
    slab2 = after(crossed[2], below1, above1)
    below2, above2 = neighbours(2, slab2)
    packed = finish(0, [slab0, below0, above0, opposite0])
    opposite1 = further(1, after(above1, packed), down)
    opposite2 = further(2, below2, up)
    finish(1, [slab1, below1, above1, after(opposite1, partials[2], arrived[0], below2)])
    finish(2, [slab2, below2, above2, opposite2])
    out = None
    for (first, last), queries in zip(CHUNKS, arrived[1:]):
        heads = last - first
        attended = attend(
            fill, cosine, sine, queries, arrived[0], cached_keys, cached_values, heads
        )
        back = exchange(attended.reshape(owners, 2, rows, heads * HEAD))
        out = unpack(pick, back, first // heads, SHARING * HEAD, out)
    return out


def solution(mesh):
    in_specs = (
        P(None, ("grp", "pair"), None),
        P("pair", "tp"),
        P("tp"),
        P(("grp", "pair", "tp"), None, None),
        P(("grp", "pair", "tp"), None, None),
        P(("grp", "pair", "tp")),
        P("grp"),
    )
    out_specs = P(None, ("grp", "pair"), "tp")
    return jax.shard_map(
        per_device, mesh=mesh, in_specs=in_specs, out_specs=out_specs, check_vma=False
    )
```

```python
import functools

import jax
import jax.numpy as jnp
from jax import lax
from jax.experimental import pallas as pl
from jax.experimental.pallas import tpu as pltpu
from jax.sharding import PartitionSpec as P

HEAD = 128
SHARING = 8
ROPE_BASE = 1000000.0
SWAP = ((0, 1), (1, 0))
CHUNKS = ((0, 4), (4, 8))
ROW_BLOCK = 8
NT = (((1,), (1,)), ((), ()))


def in_hbm(value):
    return pltpu.with_memory_space_constraint(value, pltpu.HBM)


def rope_tables(positions):
    frequency = ROPE_BASE ** (-jnp.arange(0, HEAD, 2, dtype=jnp.float32) / HEAD)
    angles = positions.astype(jnp.float32)[..., None] * frequency
    cosine = jnp.cos(angles)
    sine = jnp.sin(angles)
    return jnp.concatenate([cosine, cosine], -1), jnp.concatenate([-sine, sine], -1)


def project_kernel(owners, rows, places_ref, x_ref, *refs):
    slabs = refs[:-7]
    partial_ref, pack_ref, out_ref, taken, met, total, arrived = refs[-7:]
    depth = slabs[0].shape[0]
    share = pack_ref.shape[1]
    copies = []
    for i, slab in enumerate(slabs):
        first = pl.multiple_of(places_ref[i] * depth, depth)
        copies.append((
            pltpu.make_async_copy(x_ref.at[:, pl.ds(first, depth)], taken.at[i], arrived.at[0, i]),
            pltpu.make_async_copy(slab, met.at[i], arrived.at[1, i]),
        ))
        for copy in copies[i]:
            copy.start()
    for i in range(len(slabs)):
        for copy in copies[i]:
            copy.wait()
        product = jnp.dot(taken[i], met[i], preferred_element_type=jnp.float32)
        if i == 0:
            total[...] = partial_ref[...] + product
        else:
            total[...] += product
    for step in range(2):
        rounded = total[pl.ds(step * share, share), :].astype(jnp.bfloat16)
        packed = jnp.dot(pack_ref[...], rounded, preferred_element_type=jnp.float32)
        for owner in range(owners):
            block = packed[owner * rows:(owner + 1) * rows]
            out_ref[owner, step] = block.astype(jnp.bfloat16)


def project(places, signals, slabs, partial, pack, owners):
    lines, _ = signals.shape
    depth, wide = slabs[0].shape
    slots, share = pack.shape
    rows = slots // owners
    count = len(slabs)
    return pl.pallas_call(
        functools.partial(project_kernel, owners, rows),
        out_shape=pltpu.HBM((owners, 2, rows, wide), jnp.bfloat16),
        grid_spec=pltpu.PrefetchScalarGridSpec(
            num_scalar_prefetch=1,
            grid=(1,),
            in_specs=[pl.BlockSpec(memory_space=pl.ANY)] * (count + 1) + [
                pl.BlockSpec((lines, wide), lambda k, s: (0, 0)),
                pl.BlockSpec((slots, share), lambda k, s: (0, 0)),
            ],
            out_specs=pl.BlockSpec((owners, 2, rows, wide), lambda k, s: (0, 0, 0, 0)),
            scratch_shapes=[
                pltpu.VMEM((count, lines, depth), jnp.bfloat16),
                pltpu.VMEM((count, depth, wide), jnp.bfloat16),
                pltpu.VMEM((lines, wide), jnp.float32),
                pltpu.SemaphoreType.DMA((2, count)),
            ],
        ),
        compiler_params=pltpu.CompilerParams(vmem_limit_bytes=26 << 20),
        cost_estimate=pl.CostEstimate(
            flops=2 * lines * depth * count * wide,
            transcendentals=0,
            bytes_accessed=2 * (lines + wide) * depth * count,
        ),
    )(places, in_hbm(signals), *(in_hbm(slab) for slab in slabs), in_hbm(partial), in_hbm(pack))


def attention_kernel(heads, fill_ref, cos_ref, sin_ref, q_ref, k_new_ref, v_new_ref, k_ref, v_ref, out_ref,
                     q_rot, k_rot, v_new, cached_scores, new_scores, blended):
    n_tp = q_ref.shape[1]
    block = ROW_BLOCK
    scale = HEAD ** (-0.5)
    width = 2 * heads
    first = pl.program_id(0) * block
    size = block * width

    def both(ref, t, step, start):
        lanes = slice(start, start + HEAD)
        return ref[0, t, step, :, lanes].astype(jnp.float32) + ref[1, t, step, :, lanes].astype(jnp.float32)

    def turned(values, step):
        turn = values * cos_ref[step] + pltpu.roll(values, HEAD // 2, 1) * sin_ref[step]
        return turn.astype(jnp.bfloat16).astype(jnp.float32)

    place = lax.broadcasted_iota(jnp.int32, (width, HEAD), 1)
    line = lax.broadcasted_iota(jnp.int32, (size, 2 * block), 0)
    column = lax.broadcasted_iota(jnp.int32, (size, 2 * block), 1)
    seen = ((column % block) == (line // width)) & (
        (column < block) | (line % width >= heads)
    )
    filled = [place < fill_ref[first + i] for i in range(block)]

    for t in range(n_tp):
        for step in range(2):
            for head in range(heads):
                at = pl.ds(t * size + (step * heads + head) * block, block)
                q_rot[at, :] = turned(both(q_ref, t, step, head * HEAD), step)
            at = pl.ds(step * block, block)
            k_rot[t, at, :] = turned(both(k_new_ref, t, step, 0), step)
            v_new[t, at, :] = both(v_new_ref, t, step, 0)
    for t in range(n_tp):
        lanes = slice(t * HEAD, (t + 1) * HEAD)
        queries = [
            q_rot[pl.ds(t * size + i, width, stride=block), :].astype(jnp.bfloat16) for i in range(block)
        ]
        for i in range(block):
            scores = lax.dot_general(
                queries[i], k_ref[i, :, lanes], NT, preferred_element_type=jnp.float32
            ) * scale
            cached_scores[t, pl.ds(i * width, width), :] = jnp.where(filled[i], scores, -1e30)
        scores = lax.dot_general(
            jnp.concatenate(queries, 0), k_rot[t].astype(jnp.bfloat16), NT,
            preferred_element_type=jnp.float32,
        ) * scale
        new_scores[t] = jnp.where(seen, scores, -1e30)
    for t in range(n_tp):
        lanes = slice(t * HEAD, (t + 1) * HEAD)
        cached, new = cached_scores[t], new_scores[t]
        top = jnp.maximum(jnp.max(cached, -1, keepdims=True), jnp.max(new, -1, keepdims=True))
        cached, new = jnp.exp(cached - top), jnp.exp(new - top)
        share = 1.0 / (jnp.sum(cached, -1, keepdims=True) + jnp.sum(new, -1, keepdims=True))
        cached, new = (cached * share).astype(jnp.bfloat16), (new * share).astype(jnp.bfloat16)
        from_new = jnp.dot(new, v_new[t].astype(jnp.bfloat16), preferred_element_type=jnp.float32)
        for i in range(block):
            part = slice(i * width, (i + 1) * width)
            mixed = jnp.dot(cached[part], v_ref[i, :, lanes], preferred_element_type=jnp.float32)
            blended[pl.ds(t * size + i, width, stride=block), :] = mixed + from_new[part]
    for t in range(n_tp):
        for step in range(2):
            for head in range(heads):
                at = pl.ds(t * size + (step * heads + head) * block, block)
                done = blended[at, :].astype(jnp.bfloat16)
                for pair in range(2):
                    out_ref[pair, t, step, :, head * HEAD:(head + 1) * HEAD] = done


def attend(fill, cosine, sine, queries, new, keys, values, heads):
    _, n_tp, _, rows, _ = queries.shape
    places = keys.shape[1]
    block = ROW_BLOCK
    width = 2 * heads * block
    table = pl.BlockSpec((2, block, HEAD), lambda r, f: (0, r, 0))
    cache = pl.BlockSpec((block, places, n_tp * HEAD), lambda r, f: (r, 0, 0))

    def routed(columns, at=0):
        return pl.BlockSpec((2, n_tp, 2, block, columns), lambda r, f: (0, 0, 0, r, at))

    return pl.pallas_call(
        functools.partial(attention_kernel, heads),
        out_shape=pltpu.HBM((2, n_tp, 2, rows, heads * HEAD), jnp.bfloat16),
        grid_spec=pltpu.PrefetchScalarGridSpec(
            num_scalar_prefetch=1,
            grid=(rows // block,),
            in_specs=[
                table, table, routed(heads * HEAD), routed(HEAD, 0), routed(HEAD, 1),
                cache, cache,
            ],
            out_specs=routed(heads * HEAD),
            scratch_shapes=[
                pltpu.VMEM((n_tp * width, HEAD), jnp.float32),
                pltpu.VMEM((n_tp, 2 * block, HEAD), jnp.float32),
                pltpu.VMEM((n_tp, 2 * block, HEAD), jnp.float32),
                pltpu.VMEM((n_tp, width, HEAD), jnp.float32),
                pltpu.VMEM((n_tp, width, 2 * block), jnp.float32),
                pltpu.VMEM((n_tp * width, HEAD), jnp.float32),
            ],
        ),
        compiler_params=pltpu.CompilerParams(vmem_limit_bytes=18 << 20),
        cost_estimate=pl.CostEstimate(
            flops=8 * heads * rows * n_tp * places * HEAD,
            transcendentals=2 * heads * rows * n_tp * places,
            bytes_accessed=4 * rows * places * n_tp * HEAD,
        ),
    )(
        fill, cosine, sine, in_hbm(queries), in_hbm(new), in_hbm(new), in_hbm(keys), in_hbm(values)
    )


def unpack_kernel(owners, rows, pick_ref, back_ref, *refs):
    out_ref, gathered = refs[-2:]
    for owner in range(owners):
        gathered[pl.ds(owner * rows, rows), :] = back_ref[owner, 0].astype(jnp.float32)
    picked = jnp.dot(
        pick_ref[...], gathered[...].astype(jnp.bfloat16), preferred_element_type=jnp.float32
    )
    out_ref[0] = picked.astype(jnp.bfloat16)


def unpack(pick, back, at, columns, so_far):
    owners, _, rows, wide = back.shape
    share, slots = pick.shape
    before = [] if so_far is None else [so_far]
    return pl.pallas_call(
        functools.partial(unpack_kernel, owners, rows),
        out_shape=jax.ShapeDtypeStruct((2, share, columns), jnp.bfloat16),
        grid=(2,),
        in_specs=[
            pl.BlockSpec((share, slots), lambda s: (0, 0)),
            pl.BlockSpec((owners, 1, rows, wide), lambda s: (0, s, 0, 0)),
        ] + [pl.BlockSpec(memory_space=pl.ANY)] * len(before),
        out_specs=pl.BlockSpec((1, share, wide), lambda s: (s, 0, at)),
        scratch_shapes=[pltpu.VMEM((slots, wide), jnp.float32)],
        input_output_aliases={2: 0} if before else {},
        compiler_params=pltpu.CompilerParams(vmem_limit_bytes=8 << 20),
        cost_estimate=pl.CostEstimate(
            flops=4 * share * slots * wide, transcendentals=0, bytes_accessed=4 * slots * wide
        ),
    )(pick, back, *before)


def per_device(signals, matrix, offset, cached_keys, cached_values, fill, lines):
    n_pair, n_tp, n_grp = (int(lax.axis_size(a)) for a in ("pair", "tp", "grp"))
    pair, grp = (lax.axis_index(a) for a in ("pair", "grp"))
    share, features = signals.shape[1:]
    half, columns = matrix.shape
    rows = fill.shape[0]
    owners = n_pair * n_tp
    depth = half // n_grp

    def after(value, *earlier):
        return lax.optimization_barrier((value, *earlier))[0]

    flat = signals.reshape(2 * share, features)
    listed = lax.dynamic_slice_in_dim(lines, pair * share, share)
    slots = jnp.arange(owners * rows, dtype=jnp.int32)
    pack = (slots[:, None] == listed[None, :]).astype(jnp.bfloat16)
    pick = (listed[:, None] == slots[None, :]).astype(jnp.bfloat16)
    positions = fill[None, :] + jnp.arange(2, dtype=jnp.int32)[:, None]
    cosine, sine = rope_tables(positions)

    def exchange(blocks):
        return lax.all_to_all(blocks, ("pair", "tp"), split_axis=0, concat_axis=0, tiled=True)

    spans = [(SHARING * HEAD, columns)] + [(a * HEAD, b * HEAD) for a, b in CHUNKS]
    n_z = n_grp // 2
    up = [(2 * a + c, 2 * ((a + 1) % n_z) + c) for a in range(n_z) for c in range(2)]
    down = [(d, s) for s, d in up]
    twin = [(2 * a + c, 2 * a + 1 - c) for a in range(n_z) for c in range(2)]
    z, core = grp // 2, grp % 2
    turns = (0, n_z - 1, 1, 2)
    places = (1 - pair) * n_grp + jnp.stack(
        [(z + turn) % n_z * 2 + core for turn in turns]
        + [(z + turn) % n_z * 2 + 1 - core for turn in turns]
    )
    places = places.astype(jnp.int32)

    near = lax.dynamic_slice_in_dim(flat, pair * half, half, 1)
    partials = [
        jnp.dot(near, matrix[:, slice(*span)], preferred_element_type=jnp.float32)
        + offset[slice(*span)].astype(jnp.float32)
        for span in spans
    ]

    crossed = []
    for number, (start, stop) in enumerate(spans):
        with jax.named_scope("over_pair_%d" % number):
            slab = lax.dynamic_slice(matrix, (grp * depth, start), (depth, stop - start))
            crossed.append(lax.ppermute(after(slab, *crossed[-1:]), "pair", SWAP))
    def neighbours(number, slab):
        with jax.named_scope("from_below_%d" % number):
            below = lax.ppermute(slab, "grp", up)
        with jax.named_scope("from_above_%d" % number):
            return below, lax.ppermute(slab, "grp", down)

    def further(number, piece, way):
        with jax.named_scope("from_opposite_%d" % number):
            return lax.ppermute(piece, "grp", way)

    arrived = []

    def finish(number, four, *earlier):
        with jax.named_scope("from_twin_%d" % number):
            slabs = four + [lax.ppermute(piece, "grp", twin) for piece in four]
        with jax.named_scope("project_%d" % number):
            packed = project(places, flat, slabs, partials[number], pack, owners)
        with jax.named_scope("route_%d" % number):
            start, stop = spans[number]
            arrived.append(
                exchange(after(packed, *earlier)).reshape(n_pair, n_tp, 2, rows, stop - start)
            )
        return packed

    slab0 = after(crossed[0], partials[0])
    below0, above0 = neighbours(0, slab0)
    opposite0 = further(0, below0, up)
    slab1 = after(crossed[1], partials[1], below0, above0, opposite0)
    below1, above1 = neighbours(1, slab1)
    slab2 = after(crossed[2], below1, above1)
    below2, above2 = neighbours(2, slab2)
    packed = finish(0, [slab0, below0, above0, opposite0], below1, above1, slab2)
    opposite1 = further(1, after(above1, packed), down)
    opposite2 = further(2, below2, up)
    finish(1, [slab1, below1, above1, after(opposite1, partials[2], arrived[0], below2)])
    finish(2, [slab2, below2, above2, opposite2])
    out = None
    for (first, last), queries in zip(CHUNKS, arrived[1:]):
        heads = last - first
        attended = attend(
            fill, cosine, sine, queries, arrived[0], cached_keys, cached_values, heads
        )
        back = exchange(attended.reshape(owners, 2, rows, heads * HEAD))
        out = unpack(pick, back, first // heads, SHARING * HEAD, out)
    return out


def solution(mesh):
    in_specs = (
        P(None, ("grp", "pair"), None),
        P("pair", "tp"),
        P("tp"),
        P(("grp", "pair", "tp"), None, None),
        P(("grp", "pair", "tp"), None, None),
        P(("grp", "pair", "tp")),
        P("grp"),
    )
    out_specs = P(None, ("grp", "pair"), "tp")
    return jax.shard_map(
        per_device, mesh=mesh, in_specs=in_specs, out_specs=out_specs, check_vma=False
    )
```

```python
import functools

import jax
import jax.numpy as jnp
from jax import lax
from jax.experimental import pallas as pl
from jax.experimental.pallas import tpu as pltpu
from jax.sharding import PartitionSpec as P

HEAD = 128
SHARING = 8
ROPE_BASE = 1000000.0
SWAP = ((0, 1), (1, 0))
CHUNKS = ((0, 3), (3, 8))
ROW_BLOCK = 8
NT = (((1,), (1,)), ((), ()))


def in_hbm(value):
    return pltpu.with_memory_space_constraint(value, pltpu.HBM)


def rope_tables(positions):
    frequency = ROPE_BASE ** (-jnp.arange(0, HEAD, 2, dtype=jnp.float32) / HEAD)
    angles = positions.astype(jnp.float32)[..., None] * frequency
    cosine = jnp.cos(angles)
    sine = jnp.sin(angles)
    return jnp.concatenate([cosine, cosine], -1), jnp.concatenate([-sine, sine], -1)


def project_kernel(owners, rows, places_ref, x_ref, *refs):
    slabs = refs[:-7]
    partial_ref, pack_ref, out_ref, taken, met, total, arrived = refs[-7:]
    depth = slabs[0].shape[0]
    share = pack_ref.shape[1]
    copies = []
    for i, slab in enumerate(slabs):
        first = pl.multiple_of(places_ref[i] * depth, depth)
        copies.append((
            pltpu.make_async_copy(x_ref.at[:, pl.ds(first, depth)], taken.at[i], arrived.at[0, i]),
            pltpu.make_async_copy(slab, met.at[i], arrived.at[1, i]),
        ))
        for copy in copies[i]:
            copy.start()
    for i in range(len(slabs)):
        for copy in copies[i]:
            copy.wait()
        product = jnp.dot(taken[i], met[i], preferred_element_type=jnp.float32)
        if i == 0:
            total[...] = partial_ref[...] + product
        else:
            total[...] += product
    for step in range(2):
        rounded = total[pl.ds(step * share, share), :].astype(jnp.bfloat16)
        packed = jnp.dot(pack_ref[...], rounded, preferred_element_type=jnp.float32)
        for owner in range(owners):
            block = packed[owner * rows:(owner + 1) * rows]
            out_ref[owner, step] = block.astype(jnp.bfloat16)


def project(places, signals, slabs, partial, pack, owners):
    lines, _ = signals.shape
    depth, wide = slabs[0].shape
    slots, share = pack.shape
    rows = slots // owners
    count = len(slabs)
    return pl.pallas_call(
        functools.partial(project_kernel, owners, rows),
        out_shape=pltpu.HBM((owners, 2, rows, wide), jnp.bfloat16),
        grid_spec=pltpu.PrefetchScalarGridSpec(
            num_scalar_prefetch=1,
            grid=(1,),
            in_specs=[pl.BlockSpec(memory_space=pl.ANY)] * (count + 1) + [
                pl.BlockSpec((lines, wide), lambda k, s: (0, 0)),
                pl.BlockSpec((slots, share), lambda k, s: (0, 0)),
            ],
            out_specs=pl.BlockSpec((owners, 2, rows, wide), lambda k, s: (0, 0, 0, 0)),
            scratch_shapes=[
                pltpu.VMEM((count, lines, depth), jnp.bfloat16),
                pltpu.VMEM((count, depth, wide), jnp.bfloat16),
                pltpu.VMEM((lines, wide), jnp.float32),
                pltpu.SemaphoreType.DMA((2, count)),
            ],
        ),
        compiler_params=pltpu.CompilerParams(vmem_limit_bytes=26 << 20),
        cost_estimate=pl.CostEstimate(
            flops=2 * lines * depth * count * wide,
            transcendentals=0,
            bytes_accessed=2 * (lines + wide) * depth * count,
        ),
    )(places, in_hbm(signals), *(in_hbm(slab) for slab in slabs), in_hbm(partial), in_hbm(pack))


def attention_kernel(heads, fill_ref, cos_ref, sin_ref, q_ref, k_new_ref, v_new_ref, k_ref, v_ref, out_ref,
                     q_rot, k_rot, v_new, cached_scores, new_scores, blended):
    n_tp = q_ref.shape[1]
    block = ROW_BLOCK
    scale = HEAD ** (-0.5)
    width = 2 * heads
    first = pl.program_id(0) * block
    size = block * width

    def both(ref, t, step, start):
        lanes = slice(start, start + HEAD)
        return ref[0, t, step, :, lanes].astype(jnp.float32) + ref[1, t, step, :, lanes].astype(jnp.float32)

    def turned(values, step):
        turn = values * cos_ref[step] + pltpu.roll(values, HEAD // 2, 1) * sin_ref[step]
        return turn.astype(jnp.bfloat16).astype(jnp.float32)

    place = lax.broadcasted_iota(jnp.int32, (width, HEAD), 1)
    line = lax.broadcasted_iota(jnp.int32, (size, 2 * block), 0)
    column = lax.broadcasted_iota(jnp.int32, (size, 2 * block), 1)
    seen = ((column % block) == (line // width)) & (
        (column < block) | (line % width >= heads)
    )
    filled = [place < fill_ref[first + i] for i in range(block)]

    for t in range(n_tp):
        for step in range(2):
            for head in range(heads):
                at = pl.ds(t * size + (step * heads + head) * block, block)
                q_rot[at, :] = turned(both(q_ref, t, step, head * HEAD), step)
            at = pl.ds(step * block, block)
            k_rot[t, at, :] = turned(both(k_new_ref, t, step, 0), step)
            v_new[t, at, :] = both(v_new_ref, t, step, 0)
    for t in range(n_tp):
        lanes = slice(t * HEAD, (t + 1) * HEAD)
        queries = [
            q_rot[pl.ds(t * size + i, width, stride=block), :].astype(jnp.bfloat16) for i in range(block)
        ]
        for i in range(block):
            scores = lax.dot_general(
                queries[i], k_ref[i, :, lanes], NT, preferred_element_type=jnp.float32
            ) * scale
            cached_scores[t, pl.ds(i * width, width), :] = jnp.where(filled[i], scores, -1e30)
        scores = lax.dot_general(
            jnp.concatenate(queries, 0), k_rot[t].astype(jnp.bfloat16), NT,
            preferred_element_type=jnp.float32,
        ) * scale
        new_scores[t] = jnp.where(seen, scores, -1e30)
    for t in range(n_tp):
        lanes = slice(t * HEAD, (t + 1) * HEAD)
        cached, new = cached_scores[t], new_scores[t]
        top = jnp.maximum(jnp.max(cached, -1, keepdims=True), jnp.max(new, -1, keepdims=True))
        cached, new = jnp.exp(cached - top), jnp.exp(new - top)
        share = 1.0 / (jnp.sum(cached, -1, keepdims=True) + jnp.sum(new, -1, keepdims=True))
        cached, new = (cached * share).astype(jnp.bfloat16), (new * share).astype(jnp.bfloat16)
        from_new = jnp.dot(new, v_new[t].astype(jnp.bfloat16), preferred_element_type=jnp.float32)
        for i in range(block):
            part = slice(i * width, (i + 1) * width)
            mixed = jnp.dot(cached[part], v_ref[i, :, lanes], preferred_element_type=jnp.float32)
            blended[pl.ds(t * size + i, width, stride=block), :] = mixed + from_new[part]
    for t in range(n_tp):
        for step in range(2):
            for head in range(heads):
                at = pl.ds(t * size + (step * heads + head) * block, block)
                done = blended[at, :].astype(jnp.bfloat16)
                for pair in range(2):
                    out_ref[pair, t, step, :, head * HEAD:(head + 1) * HEAD] = done


def attend(fill, cosine, sine, queries, new, keys, values, heads):
    _, n_tp, _, rows, _ = queries.shape
    places = keys.shape[1]
    block = ROW_BLOCK
    width = 2 * heads * block
    table = pl.BlockSpec((2, block, HEAD), lambda r, f: (0, r, 0))
    cache = pl.BlockSpec((block, places, n_tp * HEAD), lambda r, f: (r, 0, 0))

    def routed(columns, at=0):
        return pl.BlockSpec((2, n_tp, 2, block, columns), lambda r, f: (0, 0, 0, r, at))

    return pl.pallas_call(
        functools.partial(attention_kernel, heads),
        out_shape=pltpu.HBM((2, n_tp, 2, rows, heads * HEAD), jnp.bfloat16),
        grid_spec=pltpu.PrefetchScalarGridSpec(
            num_scalar_prefetch=1,
            grid=(rows // block,),
            in_specs=[
                table, table, routed(heads * HEAD), routed(HEAD, 0), routed(HEAD, 1),
                cache, cache,
            ],
            out_specs=routed(heads * HEAD),
            scratch_shapes=[
                pltpu.VMEM((n_tp * width, HEAD), jnp.float32),
                pltpu.VMEM((n_tp, 2 * block, HEAD), jnp.float32),
                pltpu.VMEM((n_tp, 2 * block, HEAD), jnp.float32),
                pltpu.VMEM((n_tp, width, HEAD), jnp.float32),
                pltpu.VMEM((n_tp, width, 2 * block), jnp.float32),
                pltpu.VMEM((n_tp * width, HEAD), jnp.float32),
            ],
        ),
        compiler_params=pltpu.CompilerParams(vmem_limit_bytes=18 << 20),
        cost_estimate=pl.CostEstimate(
            flops=8 * heads * rows * n_tp * places * HEAD,
            transcendentals=2 * heads * rows * n_tp * places,
            bytes_accessed=4 * rows * places * n_tp * HEAD,
        ),
    )(
        fill, cosine, sine, in_hbm(queries), in_hbm(new), in_hbm(new), in_hbm(keys), in_hbm(values)
    )


def unpack_kernel(owners, rows, at, pick_ref, back_ref, *refs):
    out_ref, gathered, picked, written = refs[-4:]
    step = pl.program_id(0)
    for owner in range(owners):
        gathered[pl.ds(owner * rows, rows), :] = back_ref[owner, 0].astype(jnp.float32)
    picked[step] = jnp.dot(
        pick_ref[...], gathered[...].astype(jnp.bfloat16), preferred_element_type=jnp.float32
    ).astype(jnp.bfloat16)
    columns = pl.ds(at, picked.shape[2])
    copies = [
        pltpu.make_async_copy(picked.at[i], out_ref.at[i, :, columns], written.at[i])
        for i in range(2)
    ]

    @pl.when(step == 0)
    def _():
        copies[0].start()

    @pl.when(step == 1)
    def _():
        copies[1].start()
        copies[0].wait()
        copies[1].wait()


def unpack(pick, back, at, columns, so_far):
    owners, _, rows, wide = back.shape
    share, slots = pick.shape
    before = [] if so_far is None else [so_far]
    return pl.pallas_call(
        functools.partial(unpack_kernel, owners, rows, at),
        out_shape=jax.ShapeDtypeStruct((2, share, columns), jnp.bfloat16),
        grid=(2,),
        in_specs=[
            pl.BlockSpec((share, slots), lambda s: (0, 0)),
            pl.BlockSpec((owners, 1, rows, wide), lambda s: (0, s, 0, 0)),
        ] + [pl.BlockSpec(memory_space=pl.ANY)] * len(before),
        out_specs=pl.BlockSpec(memory_space=pl.ANY),
        scratch_shapes=[
            pltpu.VMEM((slots, wide), jnp.float32),
            pltpu.VMEM((2, share, wide), jnp.bfloat16),
            pltpu.SemaphoreType.DMA((2,)),
        ],
        input_output_aliases={2: 0} if before else {},
        compiler_params=pltpu.CompilerParams(vmem_limit_bytes=12 << 20),
        cost_estimate=pl.CostEstimate(
            flops=4 * share * slots * wide, transcendentals=0, bytes_accessed=4 * slots * wide
        ),
    )(pick, back, *before)


def per_device(signals, matrix, offset, cached_keys, cached_values, fill, lines):
    n_pair, n_tp, n_grp = (int(lax.axis_size(a)) for a in ("pair", "tp", "grp"))
    pair, grp = (lax.axis_index(a) for a in ("pair", "grp"))
    share, features = signals.shape[1:]
    half, columns = matrix.shape
    rows = fill.shape[0]
    owners = n_pair * n_tp
    depth = half // n_grp

    def after(value, *earlier):
        return lax.optimization_barrier((value, *earlier))[0]

    flat = signals.reshape(2 * share, features)
    listed = lax.dynamic_slice_in_dim(lines, pair * share, share)
    slots = jnp.arange(owners * rows, dtype=jnp.int32)
    pack = (slots[:, None] == listed[None, :]).astype(jnp.bfloat16)
    pick = (listed[:, None] == slots[None, :]).astype(jnp.bfloat16)
    positions = fill[None, :] + jnp.arange(2, dtype=jnp.int32)[:, None]
    cosine, sine = rope_tables(positions)

    def exchange(blocks):
        return lax.all_to_all(blocks, ("pair", "tp"), split_axis=0, concat_axis=0, tiled=True)

    spans = [(SHARING * HEAD, columns)] + [(a * HEAD, b * HEAD) for a, b in CHUNKS]
    n_z = n_grp // 2
    up = [(2 * a + c, 2 * ((a + 1) % n_z) + c) for a in range(n_z) for c in range(2)]
    down = [(d, s) for s, d in up]
    twin = [(2 * a + c, 2 * a + 1 - c) for a in range(n_z) for c in range(2)]
    z, core = grp // 2, grp % 2
    turns = (0, n_z - 1, 1, 2)
    places = (1 - pair) * n_grp + jnp.stack(
        [(z + turn) % n_z * 2 + core for turn in turns]
        + [(z + turn) % n_z * 2 + 1 - core for turn in turns]
    )
    places = places.astype(jnp.int32)

    near = lax.dynamic_slice_in_dim(flat, pair * half, half, 1)
    def against_own(span, bias):
        columns = slice(*span)
        product = jnp.dot(near, matrix[:, columns], preferred_element_type=jnp.float32)
        return product + bias[columns].astype(jnp.float32)

    crossed = []
    for number, (start, stop) in enumerate(spans):
        with jax.named_scope("over_pair_%d" % number):
            slab = lax.dynamic_slice(matrix, (grp * depth, start), (depth, stop - start))
            crossed.append(lax.ppermute(after(slab, *crossed[-1:]), "pair", SWAP))
    def neighbours(number, slab):
        with jax.named_scope("from_below_%d" % number):
            below = lax.ppermute(slab, "grp", up)
        with jax.named_scope("from_above_%d" % number):
            return below, lax.ppermute(slab, "grp", down)

    def further(number, piece, way):
        with jax.named_scope("from_opposite_%d" % number):
            return lax.ppermute(piece, "grp", way)

    arrived = []

    def finish(number, four, *earlier):
        with jax.named_scope("from_twin_%d" % number):
            slabs = four + [lax.ppermute(piece, "grp", twin) for piece in four]
        with jax.named_scope("project_%d" % number):
            packed = project(places, flat, slabs, partials[number], pack, owners)
        with jax.named_scope("route_%d" % number):
            start, stop = spans[number]
            arrived.append(
                exchange(after(packed, *earlier)).reshape(n_pair, n_tp, 2, rows, stop - start)
            )
        return packed

    longest = against_own(spans[2], offset)
    slab0 = after(crossed[0], longest)
    below0, above0 = neighbours(0, slab0)
    later = after(offset, below0)
    partials = [against_own(spans[0], later), against_own(spans[1], later)]
    partials.append(longest)
    opposite0 = further(0, below0, up)
    slab1 = after(crossed[1], partials[0], partials[1], below0, above0, opposite0)
    below1, above1 = neighbours(1, slab1)
    packed = finish(0, [slab0, below0, above0, opposite0], below1, above1)
    slab2 = after(crossed[2], below1, above1, packed, partials[2])
    below2, above2 = neighbours(2, slab2)
    opposite1 = further(1, after(above1, packed), down)
    opposite2 = further(2, after(below2, arrived[0]), up)
    finish(1, [slab1, below1, above1, after(opposite1, below2)])
    finish(2, [slab2, below2, above2, opposite2])
    out = None
    for (first, last), queries in zip(CHUNKS, arrived[1:]):
        heads = last - first
        attended = attend(
            fill, cosine, sine, queries, arrived[0], cached_keys, cached_values, heads
        )
        back = exchange(attended.reshape(owners, 2, rows, heads * HEAD))
        out = unpack(pick, back, first * HEAD, SHARING * HEAD, out)
    return out


def solution(mesh):
    in_specs = (
        P(None, ("grp", "pair"), None),
        P("pair", "tp"),
        P("tp"),
        P(("grp", "pair", "tp"), None, None),
        P(("grp", "pair", "tp"), None, None),
        P(("grp", "pair", "tp")),
        P("grp"),
    )
    out_specs = P(None, ("grp", "pair"), "tp")
    return jax.shard_map(
        per_device, mesh=mesh, in_specs=in_specs, out_specs=out_specs, check_vma=False
    )
```

```python
import functools

import jax
import jax.numpy as jnp
from jax import lax
from jax.experimental import pallas as pl
from jax.experimental.pallas import tpu as pltpu
from jax.sharding import PartitionSpec as P

HEAD = 128
SHARING = 8
ROPE_BASE = 1000000.0
SWAP = ((0, 1), (1, 0))
CHUNKS = ((0, 4), (4, 8))
ROW_BLOCK = 8
NT = (((1,), (1,)), ((), ()))


def in_hbm(value):
    return pltpu.with_memory_space_constraint(value, pltpu.HBM)


def rope_tables(positions):
    frequency = ROPE_BASE ** (-jnp.arange(0, HEAD, 2, dtype=jnp.float32) / HEAD)
    angles = positions.astype(jnp.float32)[..., None] * frequency
    cosine = jnp.cos(angles)
    sine = jnp.sin(angles)
    return jnp.concatenate([cosine, cosine], -1), jnp.concatenate([-sine, sine], -1)


def project_kernel(owners, rows, places_ref, x_ref, *refs):
    slabs = refs[:-7]
    partial_ref, pack_ref, out_ref, taken, met, total, arrived = refs[-7:]
    depth = slabs[0].shape[0]
    share = pack_ref.shape[1]
    copies = []
    for i, slab in enumerate(slabs):
        first = pl.multiple_of(places_ref[i] * depth, depth)
        copies.append((
            pltpu.make_async_copy(x_ref.at[:, pl.ds(first, depth)], taken.at[i // 2, :, pl.ds(i % 2 * depth, depth)], arrived.at[0, i]),
            pltpu.make_async_copy(slab, met.at[i // 2, pl.ds(i % 2 * depth, depth)], arrived.at[1, i]),
        ))
        for copy in copies[i]:
            copy.start()
    for i in range(len(slabs) // 2):
        for copy in copies[2 * i] + copies[2 * i + 1]:
            copy.wait()
        product = jnp.dot(taken[i], met[i], preferred_element_type=jnp.float32)
        if i == 0:
            total[...] = partial_ref[...] + product
        else:
            total[...] += product
    for step in range(2):
        rounded = total[pl.ds(step * share, share), :].astype(jnp.bfloat16)
        packed = jnp.dot(pack_ref[...], rounded, preferred_element_type=jnp.float32)
        for owner in range(owners):
            block = packed[owner * rows:(owner + 1) * rows]
            out_ref[owner, step] = block.astype(jnp.bfloat16)


def project(places, signals, slabs, partial, pack, owners):
    lines, _ = signals.shape
    depth, wide = slabs[0].shape
    slots, share = pack.shape
    rows = slots // owners
    count = len(slabs)
    return pl.pallas_call(
        functools.partial(project_kernel, owners, rows),
        out_shape=pltpu.HBM((owners, 2, rows, wide), jnp.bfloat16),
        grid_spec=pltpu.PrefetchScalarGridSpec(
            num_scalar_prefetch=1,
            grid=(1,),
            in_specs=[pl.BlockSpec(memory_space=pl.ANY)] * (count + 1) + [
                pl.BlockSpec((lines, wide), lambda k, s: (0, 0)),
                pl.BlockSpec((slots, share), lambda k, s: (0, 0)),
            ],
            out_specs=pl.BlockSpec((owners, 2, rows, wide), lambda k, s: (0, 0, 0, 0)),
            scratch_shapes=[
                pltpu.VMEM((count // 2, lines, 2 * depth), jnp.bfloat16),
                pltpu.VMEM((count // 2, 2 * depth, wide), jnp.bfloat16),
                pltpu.VMEM((lines, wide), jnp.float32),
                pltpu.SemaphoreType.DMA((2, count)),
            ],
        ),
        compiler_params=pltpu.CompilerParams(vmem_limit_bytes=26 << 20),
        cost_estimate=pl.CostEstimate(
            flops=2 * lines * depth * count * wide,
            transcendentals=0,
            bytes_accessed=2 * (lines + wide) * depth * count,
        ),
    )(places, in_hbm(signals), *(in_hbm(slab) for slab in slabs), in_hbm(partial), in_hbm(pack))


def attention_kernel(heads, fill_ref, cos_ref, sin_ref, q_ref, k_new_ref, v_new_ref, k_ref, v_ref, out_ref,
                     q_rot, k_rot, v_new, cached_scores, new_scores, blended):
    n_tp = q_ref.shape[1]
    block = ROW_BLOCK
    scale = HEAD ** (-0.5)
    width = 2 * heads
    first = pl.program_id(0) * block
    size = block * width

    def both(ref, t, step, start):
        lanes = slice(start, start + HEAD)
        return ref[0, t, step, :, lanes].astype(jnp.float32) + ref[1, t, step, :, lanes].astype(jnp.float32)

    def turned(values, step):
        turn = values * cos_ref[step] + pltpu.roll(values, HEAD // 2, 1) * sin_ref[step]
        return turn.astype(jnp.bfloat16).astype(jnp.float32)

    place = lax.broadcasted_iota(jnp.int32, (width, HEAD), 1)
    line = lax.broadcasted_iota(jnp.int32, (size, 2 * block), 0)
    column = lax.broadcasted_iota(jnp.int32, (size, 2 * block), 1)
    seen = ((column % block) == (line // width)) & (
        (column < block) | (line % width >= heads)
    )
    filled = [place < fill_ref[first + i] for i in range(block)]

    for t in range(n_tp):
        for step in range(2):
            for head in range(heads):
                at = pl.ds(t * size + (step * heads + head) * block, block)
                q_rot[at, :] = turned(both(q_ref, t, step, head * HEAD), step)
            at = pl.ds(step * block, block)
            k_rot[t, at, :] = turned(both(k_new_ref, t, step, 0), step)
            v_new[t, at, :] = both(v_new_ref, t, step, 0)
    for t in range(n_tp):
        lanes = slice(t * HEAD, (t + 1) * HEAD)
        queries = [
            q_rot[pl.ds(t * size + i, width, stride=block), :].astype(jnp.bfloat16) for i in range(block)
        ]
        for i in range(block):
            scores = lax.dot_general(
                queries[i], k_ref[i, :, lanes], NT, preferred_element_type=jnp.float32
            ) * scale
            cached_scores[t, pl.ds(i * width, width), :] = jnp.where(filled[i], scores, -1e30)
        scores = lax.dot_general(
            jnp.concatenate(queries, 0), k_rot[t].astype(jnp.bfloat16), NT,
            preferred_element_type=jnp.float32,
        ) * scale
        new_scores[t] = jnp.where(seen, scores, -1e30)
    for t in range(n_tp):
        lanes = slice(t * HEAD, (t + 1) * HEAD)
        cached, new = cached_scores[t], new_scores[t]
        top = jnp.maximum(jnp.max(cached, -1, keepdims=True), jnp.max(new, -1, keepdims=True))
        cached, new = jnp.exp(cached - top), jnp.exp(new - top)
        share = 1.0 / (jnp.sum(cached, -1, keepdims=True) + jnp.sum(new, -1, keepdims=True))
        cached, new = (cached * share).astype(jnp.bfloat16), (new * share).astype(jnp.bfloat16)
        from_new = jnp.dot(new, v_new[t].astype(jnp.bfloat16), preferred_element_type=jnp.float32)
        for i in range(block):
            part = slice(i * width, (i + 1) * width)
            mixed = jnp.dot(cached[part], v_ref[i, :, lanes], preferred_element_type=jnp.float32)
            blended[pl.ds(t * size + i, width, stride=block), :] = mixed + from_new[part]
    for t in range(n_tp):
        for step in range(2):
            for head in range(heads):
                at = pl.ds(t * size + (step * heads + head) * block, block)
                done = blended[at, :].astype(jnp.bfloat16)
                for pair in range(2):
                    out_ref[pair, t, step, :, head * HEAD:(head + 1) * HEAD] = done


def attend(fill, cosine, sine, queries, new, keys, values, heads):
    _, n_tp, _, rows, _ = queries.shape
    places = keys.shape[1]
    block = ROW_BLOCK
    width = 2 * heads * block
    table = pl.BlockSpec((2, block, HEAD), lambda r, f: (0, r, 0))
    cache = pl.BlockSpec((block, places, n_tp * HEAD), lambda r, f: (r, 0, 0))

    def routed(columns, at=0):
        return pl.BlockSpec((2, n_tp, 2, block, columns), lambda r, f: (0, 0, 0, r, at))

    return pl.pallas_call(
        functools.partial(attention_kernel, heads),
        out_shape=pltpu.HBM((2, n_tp, 2, rows, heads * HEAD), jnp.bfloat16),
        grid_spec=pltpu.PrefetchScalarGridSpec(
            num_scalar_prefetch=1,
            grid=(rows // block,),
            in_specs=[
                table, table, routed(heads * HEAD), routed(HEAD, 0), routed(HEAD, 1),
                cache, cache,
            ],
            out_specs=routed(heads * HEAD),
            scratch_shapes=[
                pltpu.VMEM((n_tp * width, HEAD), jnp.float32),
                pltpu.VMEM((n_tp, 2 * block, HEAD), jnp.float32),
                pltpu.VMEM((n_tp, 2 * block, HEAD), jnp.float32),
                pltpu.VMEM((n_tp, width, HEAD), jnp.float32),
                pltpu.VMEM((n_tp, width, 2 * block), jnp.float32),
                pltpu.VMEM((n_tp * width, HEAD), jnp.float32),
            ],
        ),
        compiler_params=pltpu.CompilerParams(vmem_limit_bytes=18 << 20),
        cost_estimate=pl.CostEstimate(
            flops=8 * heads * rows * n_tp * places * HEAD,
            transcendentals=2 * heads * rows * n_tp * places,
            bytes_accessed=4 * rows * places * n_tp * HEAD,
        ),
    )(
        fill, cosine, sine, in_hbm(queries), in_hbm(new), in_hbm(new), in_hbm(keys), in_hbm(values)
    )


def unpack_kernel(owners, rows, pick_ref, back_ref, *refs):
    out_ref, gathered = refs[-2:]
    for owner in range(owners):
        gathered[pl.ds(owner * rows, rows), :] = back_ref[owner, 0].astype(jnp.float32)
    picked = jnp.dot(
        pick_ref[...], gathered[...].astype(jnp.bfloat16), preferred_element_type=jnp.float32
    )
    out_ref[0] = picked.astype(jnp.bfloat16)


def unpack(pick, back, at, columns, so_far):
    owners, _, rows, wide = back.shape
    share, slots = pick.shape
    before = [] if so_far is None else [so_far]
    return pl.pallas_call(
        functools.partial(unpack_kernel, owners, rows),
        out_shape=jax.ShapeDtypeStruct((2, share, columns), jnp.bfloat16),
        grid=(2,),
        in_specs=[
            pl.BlockSpec((share, slots), lambda s: (0, 0)),
            pl.BlockSpec((owners, 1, rows, wide), lambda s: (0, s, 0, 0)),
        ] + [pl.BlockSpec(memory_space=pl.ANY)] * len(before),
        out_specs=pl.BlockSpec((1, share, wide), lambda s: (s, 0, at)),
        scratch_shapes=[pltpu.VMEM((slots, wide), jnp.float32)],
        input_output_aliases={2: 0} if before else {},
        compiler_params=pltpu.CompilerParams(vmem_limit_bytes=8 << 20),
        cost_estimate=pl.CostEstimate(
            flops=4 * share * slots * wide, transcendentals=0, bytes_accessed=4 * slots * wide
        ),
    )(pick, back, *before)


def per_device(signals, matrix, offset, cached_keys, cached_values, fill, lines):
    n_pair, n_tp, n_grp = (int(lax.axis_size(a)) for a in ("pair", "tp", "grp"))
    pair, grp = (lax.axis_index(a) for a in ("pair", "grp"))
    share, features = signals.shape[1:]
    half, columns = matrix.shape
    rows = fill.shape[0]
    owners = n_pair * n_tp
    depth = half // n_grp

    def after(value, *earlier):
        return lax.optimization_barrier((value, *earlier))[0]

    flat = signals.reshape(2 * share, features)
    listed = lax.dynamic_slice_in_dim(lines, pair * share, share)
    slots = jnp.arange(owners * rows, dtype=jnp.int32)
    pack = (slots[:, None] == listed[None, :]).astype(jnp.bfloat16)
    pick = (listed[:, None] == slots[None, :]).astype(jnp.bfloat16)
    positions = fill[None, :] + jnp.arange(2, dtype=jnp.int32)[:, None]
    cosine, sine = rope_tables(positions)

    def exchange(blocks):
        return lax.all_to_all(blocks, ("pair", "tp"), split_axis=0, concat_axis=0, tiled=True)

    spans = [(SHARING * HEAD, columns)] + [(a * HEAD, b * HEAD) for a, b in CHUNKS]
    n_z = n_grp // 2
    up = [(2 * a + c, 2 * ((a + 1) % n_z) + c) for a in range(n_z) for c in range(2)]
    down = [(d, s) for s, d in up]
    twin = [(2 * a + c, 2 * a + 1 - c) for a in range(n_z) for c in range(2)]
    z, core = grp // 2, grp % 2
    turns = (0, n_z - 1, 1, 2)
    places = (1 - pair) * n_grp + jnp.stack(
        [(z + turn) % n_z * 2 + core for turn in turns]
        + [(z + turn) % n_z * 2 + 1 - core for turn in turns]
    )
    places = places.astype(jnp.int32)

    near = lax.dynamic_slice_in_dim(flat, pair * half, half, 1)
    partials = [
        jnp.dot(near, matrix[:, slice(*span)], preferred_element_type=jnp.float32)
        + offset[slice(*span)].astype(jnp.float32)
        for span in spans
    ]

    crossed = []
    for number, (start, stop) in enumerate(spans):
        with jax.named_scope("over_pair_%d" % number):
            slab = lax.dynamic_slice(matrix, (grp * depth, start), (depth, stop - start))
            crossed.append(lax.ppermute(after(slab, *crossed[-1:]), "pair", SWAP))
    def neighbours(number, slab):
        with jax.named_scope("from_below_%d" % number):
            below = lax.ppermute(slab, "grp", up)
        with jax.named_scope("from_above_%d" % number):
            return below, lax.ppermute(slab, "grp", down)

    def further(number, piece, way):
        with jax.named_scope("from_opposite_%d" % number):
            return lax.ppermute(piece, "grp", way)

    arrived = []

    def finish(number, four, *earlier):
        with jax.named_scope("from_twin_%d" % number):
            slabs = four + [lax.ppermute(piece, "grp", twin) for piece in four]
        with jax.named_scope("project_%d" % number):
            packed = project(places, flat, slabs, partials[number], pack, owners)
        with jax.named_scope("route_%d" % number):
            start, stop = spans[number]
            arrived.append(
                exchange(after(packed, *earlier)).reshape(n_pair, n_tp, 2, rows, stop - start)
            )
        return packed

    slab0 = after(crossed[0], partials[0])
    below0, above0 = neighbours(0, slab0)
    opposite0 = further(0, below0, up)
    slab1 = after(crossed[1], partials[1], below0, above0, opposite0)
    below1, above1 = neighbours(1, slab1)
    slab2 = after(crossed[2], below1, above1)
    below2, above2 = neighbours(2, slab2)
    packed = finish(0, [slab0, below0, above0, opposite0], below1, above1, slab2)
    opposite1 = further(1, after(above1, packed), down)
    opposite2 = further(2, below2, up)
    finish(1, [slab1, below1, above1, after(opposite1, partials[2], arrived[0], below2)])
    finish(2, [slab2, below2, above2, opposite2])
    out = None
    for (first, last), queries in zip(CHUNKS, arrived[1:]):
        heads = last - first
        attended = attend(
            fill, cosine, sine, queries, arrived[0], cached_keys, cached_values, heads
        )
        back = exchange(attended.reshape(owners, 2, rows, heads * HEAD))
        out = unpack(pick, back, first // heads, SHARING * HEAD, out)
    return out


def solution(mesh):
    in_specs = (
        P(None, ("grp", "pair"), None),
        P("pair", "tp"),
        P("tp"),
        P(("grp", "pair", "tp"), None, None),
        P(("grp", "pair", "tp"), None, None),
        P(("grp", "pair", "tp")),
        P("grp"),
    )
    out_specs = P(None, ("grp", "pair"), "tp")
    return jax.shard_map(
        per_device, mesh=mesh, in_specs=in_specs, out_specs=out_specs, check_vma=False
    )
```

```python
import functools

import jax
import jax.numpy as jnp
from jax import lax
from jax.experimental import pallas as pl
from jax.experimental.pallas import tpu as pltpu
from jax.sharding import PartitionSpec as P

HEAD = 128
SHARING = 8
ROPE_BASE = 1000000.0
SWAP = ((0, 1), (1, 0))
CHUNKS = ((0, 4), (4, 8))
ROW_BLOCK = 8
NT = (((1,), (1,)), ((), ()))


def in_hbm(value):
    return pltpu.with_memory_space_constraint(value, pltpu.HBM)


def rope_tables(positions):
    frequency = ROPE_BASE ** (-jnp.arange(0, HEAD, 2, dtype=jnp.float32) / HEAD)
    angles = positions.astype(jnp.float32)[..., None] * frequency
    cosine = jnp.cos(angles)
    sine = jnp.sin(angles)
    return jnp.concatenate([cosine, cosine], -1), jnp.concatenate([-sine, sine], -1)


def project_kernel(owners, rows, places_ref, x_ref, *refs):
    slabs = refs[:-7]
    partial_ref, pack_ref, out_ref, taken, met, total, arrived = refs[-7:]
    depth = slabs[0].shape[0]
    share = pack_ref.shape[1]
    copies = []
    for i, slab in enumerate(slabs):
        first = pl.multiple_of(places_ref[i] * depth, depth)
        copies.append((
            pltpu.make_async_copy(x_ref.at[:, pl.ds(first, depth)], taken.at[i // 2, :, pl.ds(i % 2 * depth, depth)], arrived.at[0, i]),
            pltpu.make_async_copy(slab, met.at[i // 2, pl.ds(i % 2 * depth, depth)], arrived.at[1, i]),
        ))
        for copy in copies[i]:
            copy.start()
    for i in range(len(slabs) // 2):
        for copy in copies[2 * i] + copies[2 * i + 1]:
            copy.wait()
        product = jnp.dot(taken[i], met[i], preferred_element_type=jnp.float32)
        if i == 0:
            total[...] = partial_ref[...] + product
        else:
            total[...] += product
    for step in range(2):
        rounded = total[pl.ds(step * share, share), :].astype(jnp.bfloat16)
        packed = jnp.dot(pack_ref[...], rounded, preferred_element_type=jnp.float32)
        for owner in range(owners):
            block = packed[owner * rows:(owner + 1) * rows]
            out_ref[owner, step] = block.astype(jnp.bfloat16)


def project(places, signals, slabs, partial, pack, owners):
    lines, _ = signals.shape
    depth, wide = slabs[0].shape
    slots, share = pack.shape
    rows = slots // owners
    count = len(slabs)
    return pl.pallas_call(
        functools.partial(project_kernel, owners, rows),
        out_shape=pltpu.HBM((owners, 2, rows, wide), jnp.bfloat16),
        grid_spec=pltpu.PrefetchScalarGridSpec(
            num_scalar_prefetch=1,
            grid=(1,),
            in_specs=[pl.BlockSpec(memory_space=pl.ANY)] * (count + 1) + [
                pl.BlockSpec((lines, wide), lambda k, s: (0, 0)),
                pl.BlockSpec((slots, share), lambda k, s: (0, 0)),
            ],
            out_specs=pl.BlockSpec((owners, 2, rows, wide), lambda k, s: (0, 0, 0, 0)),
            scratch_shapes=[
                pltpu.VMEM((count // 2, lines, 2 * depth), jnp.bfloat16),
                pltpu.VMEM((count // 2, 2 * depth, wide), jnp.bfloat16),
                pltpu.VMEM((lines, wide), jnp.float32),
                pltpu.SemaphoreType.DMA((2, count)),
            ],
        ),
        compiler_params=pltpu.CompilerParams(vmem_limit_bytes=26 << 20),
        cost_estimate=pl.CostEstimate(
            flops=2 * lines * depth * count * wide,
            transcendentals=0,
            bytes_accessed=2 * (lines + wide) * depth * count,
        ),
    )(places, in_hbm(signals), *(in_hbm(slab) for slab in slabs), in_hbm(partial), in_hbm(pack))


def attention_kernel(heads, fill_ref, cos_ref, sin_ref, q_ref, k_new_ref, v_new_ref, k_ref, v_ref, out_ref,
                     q_rot, k_rot, v_new, cached_scores, new_scores, blended):
    n_tp = q_ref.shape[1]
    block = ROW_BLOCK
    scale = HEAD ** (-0.5)
    width = 2 * heads
    first = pl.program_id(0) * block
    size = block * width

    def both(ref, t, step, start):
        lanes = slice(start, start + HEAD)
        return ref[0, t, step, :, lanes].astype(jnp.float32) + ref[1, t, step, :, lanes].astype(jnp.float32)

    def turned(values, step):
        turn = values * cos_ref[step] + pltpu.roll(values, HEAD // 2, 1) * sin_ref[step]
        return turn.astype(jnp.bfloat16).astype(jnp.float32)

    place = lax.broadcasted_iota(jnp.int32, (width, HEAD), 1)
    line = lax.broadcasted_iota(jnp.int32, (size, 2 * block), 0)
    column = lax.broadcasted_iota(jnp.int32, (size, 2 * block), 1)
    seen = ((column % block) == (line // width)) & (
        (column < block) | (line % width >= heads)
    )
    filled = [place < fill_ref[first + i] for i in range(block)]

    for t in range(n_tp):
        for step in range(2):
            for head in range(heads):
                at = pl.ds(t * size + (step * heads + head) * block, block)
                q_rot[at, :] = turned(both(q_ref, t, step, head * HEAD), step)
            at = pl.ds(step * block, block)
            k_rot[t, at, :] = turned(both(k_new_ref, t, step, 0), step)
            v_new[t, at, :] = both(v_new_ref, t, step, 0)
    for t in range(n_tp):
        lanes = slice(t * HEAD, (t + 1) * HEAD)
        queries = [
            q_rot[pl.ds(t * size + i, width, stride=block), :].astype(jnp.bfloat16) for i in range(block)
        ]
        for i in range(block):
            scores = lax.dot_general(
                queries[i], k_ref[i, :, lanes], NT, preferred_element_type=jnp.float32
            ) * scale
            cached_scores[t, pl.ds(i * width, width), :] = jnp.where(filled[i], scores, -1e30)
        scores = lax.dot_general(
            jnp.concatenate(queries, 0), k_rot[t].astype(jnp.bfloat16), NT,
            preferred_element_type=jnp.float32,
        ) * scale
        new_scores[t] = jnp.where(seen, scores, -1e30)
    for t in range(n_tp):
        lanes = slice(t * HEAD, (t + 1) * HEAD)
        cached, new = cached_scores[t], new_scores[t]
        top = jnp.maximum(jnp.max(cached, -1, keepdims=True), jnp.max(new, -1, keepdims=True))
        cached, new = jnp.exp(cached - top), jnp.exp(new - top)
        share = 1.0 / (jnp.sum(cached, -1, keepdims=True) + jnp.sum(new, -1, keepdims=True))
        cached, new = (cached * share).astype(jnp.bfloat16), (new * share).astype(jnp.bfloat16)
        from_new = jnp.dot(new, v_new[t].astype(jnp.bfloat16), preferred_element_type=jnp.float32)
        for i in range(block):
            part = slice(i * width, (i + 1) * width)
            mixed = jnp.dot(cached[part], v_ref[i, :, lanes], preferred_element_type=jnp.float32)
            blended[pl.ds(t * size + i, width, stride=block), :] = mixed + from_new[part]
    for t in range(n_tp):
        for step in range(2):
            for head in range(heads):
                at = pl.ds(t * size + (step * heads + head) * block, block)
                done = blended[at, :].astype(jnp.bfloat16)
                for pair in range(2):
                    out_ref[pair, t, step, :, head * HEAD:(head + 1) * HEAD] = done


def attend(fill, cosine, sine, queries, new, keys, values, heads):
    _, n_tp, _, rows, _ = queries.shape
    places = keys.shape[1]
    block = ROW_BLOCK
    width = 2 * heads * block
    table = pl.BlockSpec((2, block, HEAD), lambda r, f: (0, r, 0))
    cache = pl.BlockSpec((block, places, n_tp * HEAD), lambda r, f: (r, 0, 0))

    def routed(columns, at=0):
        return pl.BlockSpec((2, n_tp, 2, block, columns), lambda r, f: (0, 0, 0, r, at))

    return pl.pallas_call(
        functools.partial(attention_kernel, heads),
        out_shape=pltpu.HBM((2, n_tp, 2, rows, heads * HEAD), jnp.bfloat16),
        grid_spec=pltpu.PrefetchScalarGridSpec(
            num_scalar_prefetch=1,
            grid=(rows // block,),
            in_specs=[
                table, table, routed(heads * HEAD), routed(HEAD, 0), routed(HEAD, 1),
                cache, cache,
            ],
            out_specs=routed(heads * HEAD),
            scratch_shapes=[
                pltpu.VMEM((n_tp * width, HEAD), jnp.float32),
                pltpu.VMEM((n_tp, 2 * block, HEAD), jnp.float32),
                pltpu.VMEM((n_tp, 2 * block, HEAD), jnp.float32),
                pltpu.VMEM((n_tp, width, HEAD), jnp.float32),
                pltpu.VMEM((n_tp, width, 2 * block), jnp.float32),
                pltpu.VMEM((n_tp * width, HEAD), jnp.float32),
            ],
        ),
        compiler_params=pltpu.CompilerParams(vmem_limit_bytes=18 << 20),
        cost_estimate=pl.CostEstimate(
            flops=8 * heads * rows * n_tp * places * HEAD,
            transcendentals=2 * heads * rows * n_tp * places,
            bytes_accessed=4 * rows * places * n_tp * HEAD,
        ),
    )(
        fill, cosine, sine, in_hbm(queries), in_hbm(new), in_hbm(new), in_hbm(keys), in_hbm(values)
    )


def unpack_kernel(owners, rows, pick_ref, back_ref, *refs):
    out_ref, gathered = refs[-2:]
    for owner in range(owners):
        gathered[pl.ds(owner * rows, rows), :] = back_ref[owner, 0].astype(jnp.float32)
    picked = jnp.dot(
        pick_ref[...], gathered[...].astype(jnp.bfloat16), preferred_element_type=jnp.float32
    )
    out_ref[0] = picked.astype(jnp.bfloat16)


def unpack(pick, back, at, columns, so_far):
    owners, _, rows, wide = back.shape
    share, slots = pick.shape
    before = [] if so_far is None else [so_far]
    return pl.pallas_call(
        functools.partial(unpack_kernel, owners, rows),
        out_shape=jax.ShapeDtypeStruct((2, share, columns), jnp.bfloat16),
        grid=(2,),
        in_specs=[
            pl.BlockSpec((share, slots), lambda s: (0, 0)),
            pl.BlockSpec((owners, 1, rows, wide), lambda s: (0, s, 0, 0)),
        ] + [pl.BlockSpec(memory_space=pl.ANY)] * len(before),
        out_specs=pl.BlockSpec((1, share, wide), lambda s: (s, 0, at)),
        scratch_shapes=[pltpu.VMEM((slots, wide), jnp.float32)],
        input_output_aliases={2: 0} if before else {},
        compiler_params=pltpu.CompilerParams(vmem_limit_bytes=8 << 20),
        cost_estimate=pl.CostEstimate(
            flops=4 * share * slots * wide, transcendentals=0, bytes_accessed=4 * slots * wide
        ),
    )(pick, back, *before)


def per_device(signals, matrix, offset, cached_keys, cached_values, fill, lines):
    n_pair, n_tp, n_grp = (int(lax.axis_size(a)) for a in ("pair", "tp", "grp"))
    pair, grp = (lax.axis_index(a) for a in ("pair", "grp"))
    share, features = signals.shape[1:]
    half, columns = matrix.shape
    rows = fill.shape[0]
    owners = n_pair * n_tp
    depth = half // n_grp

    def after(value, *earlier):
        return lax.optimization_barrier((value, *earlier))[0]

    flat = signals.reshape(2 * share, features)
    listed = lax.dynamic_slice_in_dim(lines, pair * share, share)
    slots = jnp.arange(owners * rows, dtype=jnp.int32)
    pack = (slots[:, None] == listed[None, :]).astype(jnp.bfloat16)
    pick = (listed[:, None] == slots[None, :]).astype(jnp.bfloat16)
    positions = fill[None, :] + jnp.arange(2, dtype=jnp.int32)[:, None]
    cosine, sine = rope_tables(positions)

    def exchange(blocks):
        return lax.all_to_all(blocks, ("pair", "tp"), split_axis=0, concat_axis=0, tiled=True)

    spans = [(SHARING * HEAD, columns)] + [(a * HEAD, b * HEAD) for a, b in CHUNKS]
    n_z = n_grp // 2
    up = [(2 * a + c, 2 * ((a + 1) % n_z) + c) for a in range(n_z) for c in range(2)]
    down = [(d, s) for s, d in up]
    twin = [(2 * a + c, 2 * a + 1 - c) for a in range(n_z) for c in range(2)]
    z, core = grp // 2, grp % 2
    turns = (0, n_z - 1, 1, 2)
    places = (1 - pair) * n_grp + jnp.stack(
        [(z + turn) % n_z * 2 + core for turn in turns]
        + [(z + turn) % n_z * 2 + 1 - core for turn in turns]
    )
    places = places.astype(jnp.int32)

    near = lax.dynamic_slice_in_dim(flat, pair * half, half, 1)
    partials = [
        jnp.dot(near, matrix[:, slice(*span)], preferred_element_type=jnp.float32)
        + offset[slice(*span)].astype(jnp.float32)
        for span in spans
    ]

    crossed = []
    for number, (start, stop) in enumerate(spans):
        with jax.named_scope("over_pair_%d" % number):
            slab = lax.dynamic_slice(matrix, (grp * depth, start), (depth, stop - start))
            crossed.append(lax.ppermute(after(slab, *crossed[-1:]), "pair", SWAP))
    def neighbours(number, slab):
        with jax.named_scope("from_below_%d" % number):
            below = lax.ppermute(slab, "grp", up)
        with jax.named_scope("from_above_%d" % number):
            return below, lax.ppermute(slab, "grp", down)

    def further(number, piece, way):
        with jax.named_scope("from_opposite_%d" % number):
            return lax.ppermute(piece, "grp", way)

    arrived = []

    def finish(number, four, *earlier):
        with jax.named_scope("from_twin_%d" % number):
            slabs = four + [lax.ppermute(piece, "grp", twin) for piece in four]
        with jax.named_scope("project_%d" % number):
            packed = project(places, flat, slabs, partials[number], pack, owners)
        with jax.named_scope("route_%d" % number):
            start, stop = spans[number]
            arrived.append(
                exchange(after(packed, *earlier)).reshape(n_pair, n_tp, 2, rows, stop - start)
            )
        return packed

    slab0 = after(crossed[0], partials[0])
    below0, above0 = neighbours(0, slab0)
    opposite0 = further(0, below0, up)
    slab1 = after(crossed[1], partials[1], below0, above0, opposite0)
    below1, above1 = neighbours(1, slab1)
    slab2 = after(crossed[2], below1, above1)
    below2, above2 = neighbours(2, slab2)
    packed = finish(0, [slab0, below0, above0, opposite0], below1, above1, slab2)
    opposite1 = further(1, after(above1, packed), down)
    opposite2 = further(2, below2, up)
    finish(1, [slab1, below1, above1, after(opposite1, partials[2], below2)])
    finish(2, [slab2, below2, above2, opposite2])
    out = None
    for (first, last), queries in zip(CHUNKS, arrived[1:]):
        heads = last - first
        attended = attend(
            fill, cosine, sine, queries, arrived[0], cached_keys, cached_values, heads
        )
        back = exchange(attended.reshape(owners, 2, rows, heads * HEAD))
        out = unpack(pick, back, first // heads, SHARING * HEAD, out)
    return out


def solution(mesh):
    in_specs = (
        P(None, ("grp", "pair"), None),
        P("pair", "tp"),
        P("tp"),
        P(("grp", "pair", "tp"), None, None),
        P(("grp", "pair", "tp"), None, None),
        P(("grp", "pair", "tp")),
        P("grp"),
    )
    out_specs = P(None, ("grp", "pair"), "tp")
    return jax.shard_map(
        per_device, mesh=mesh, in_specs=in_specs, out_specs=out_specs, check_vma=False
    )
```
